32 devices in a mesh: ctx: 8 (over z, y), tp: 4 (over x, core).
Axes of the slice: x: 2, y: 2, z: 4, core: 2. Of those that a mesh axis runs over, the one named last changes fastest.
Arguments:
- tokens: bfloat16 [1024, 8192], P('ctx', 'tp'), may hold values from -6 to 6
- query_mr: bfloat16 [1024, 8192], P('ctx', 'tp'), may hold values from -6 to 6
- key_mr: bfloat16 [1024, 8192], P('ctx', 'tp'), may hold values from -6 to 6
- gain_mr: float32 [8192], P('tp'), may hold values from 0.5 to 1.5
- filter_mr: bfloat16 [512, 128], P('tp'), may hold values from -0.5 to 0.5
- query_li: bfloat16 [1024, 8192], P('ctx', 'tp'), may hold values from -6 to 6
- key_li: bfloat16 [1024, 8192], P('ctx', 'tp'), may hold values from -6 to 6
- gain_li: float32 [8192], P('tp'), may hold values from 0.5 to 1.5
- log_rates: float32 [16, 8192], P(None, 'tp'), may hold values from -12 to -3, as said below
- retain: float32 [1024], P('ctx'), may hold values from 0.6 to 1, as said below
- residues: float32 [16, 8192], P(None, 'tp'), may hold values from -1.5 to 1.5
- cotangent: bfloat16 [1024, 8192], P('ctx', 'tp'), may hold values from -6 to 6
Outputs:
- mixed: bfloat16 [1024, 8192], P('ctx', 'tp')
- grad_tokens: bfloat16 [1024, 8192], P('ctx', 'tp')
- grad_query_mr: bfloat16 [1024, 8192], P('ctx', 'tp')
- gradient_key_medium: bfloat16 [1024, 8192], P('ctx', 'tp')
- grad_query_li: bfloat16 [1024, 8192], P('ctx', 'tp')
- grad_key_li: bfloat16 [1024, 8192], P('ctx', 'tp')
- grad_gain_mr: float32 [8192], P('tp')
- grad_gain_li: float32 [8192], P('tp')
- grad_filter_mr: float32 [512, 128], P('tp')
- grad_residues: float32 [16, 8192], P(None, 'tp')
- grad_log_rates: float32 [16, 8192], P(None, 'tp')
The draws below stay inside these ranges and needn't reach their ends.
Inputs may be any that keep to these rules, and one draw needn't show every extreme that they name: `log_rates`: each entry is the logarithm of a decay rate per position. `retain`: a share of state kept at a position, 1 at most positions.
All inputs are finite; a program needn't handle non-finite values.
Results may differ from the reference program's by a relative error of at most 0.0054.
Values may be sent and summed in bfloat16 or wider, within the bound.
A program may use at most 128 MiB of HBM per device.

```python
import jax
import jax.numpy as jnp
from jax import lax

D = 8192
FILT = 128
MODES = 16
GROUP = 16
TOK_DEV = 128
WINDOW_SITES = 1024


def draw_log_rates(key, part):
    select_key, slow_key, fast_key = jax.random.split(key, 3)
    share = 0.5
    slow = jax.random.uniform(select_key, (MODES, D)) < share
    slow_log = jax.random.uniform(slow_key, (MODES, D), minval=jnp.log(0.25 / WINDOW_SITES), maxval=jnp.log(1.0 / WINDOW_SITES))
    fast_log = jax.random.uniform(fast_key, (MODES, D), minval=jnp.log(1.0 / 50.0), maxval=jnp.log(1.0 / 30.0))
    return jnp.where(slow, slow_log, fast_log).astype(jnp.float32)


def draw_retain(key, part):
    locus_random_seed, value_key = jax.random.split(key, 2)
    tile_extent = jax.random.uniform(locus_random_seed, (WINDOW_SITES,)) < 4.0 / WINDOW_SITES
    doubling_tier = jax.random.uniform(value_key, (WINDOW_SITES,), minval=0.6, maxval=0.85)
    return jnp.where(tile_extent, doubling_tier, 1.0).astype(jnp.float32)


def block_scale(own_key, extent, cuts, low, largest):
    level = 1.0
    for axis_at, shards_of in cuts:
        draws = jax.random.uniform(jax.random.fold_in(jax.random.fold_in(own_key, 6), axis_at), (shards_of,), jnp.float32, low / len(cuts), largest / len(cuts))
        level = level * jnp.repeat(jnp.exp(draws), extent[axis_at] // shards_of).reshape((-1,) + (1,) * (len(extent) - 1 - axis_at))
    return level


def bell_draw(key, shape, spread, reach, cuts=(), kind=jnp.bfloat16):
    values = jax.random.normal(key, shape, jnp.float32) * spread
    if len(cuts) > 0:
        values = block_scale(key, shape, cuts, -0.22, 0.18) * values
    return jnp.clip(values, min=-reach, max=reach).astype(kind)


def setup_inputs(seed: int = 0) -> dict:
    seeds = jax.random.split(jax.random.key(seed), 13)
    tokens = bell_draw(seeds[0], (WINDOW_SITES, D), 1.0, 6.0, ((0, 8), (1, 4)))
    query_mr = bell_draw(seeds[1], (WINDOW_SITES, D), 1.0, 6.0, ((0, 8), (1, 4)))
    key_mr = bell_draw(seeds[2], (WINDOW_SITES, D), 1.0, 6.0, ((0, 8), (1, 4)))
    gain_mr = jnp.clip(1.0 + 0.1 * jax.random.normal(seeds[3], (D,), jnp.float32), 0.5, 1.5)
    filter_mr = bell_draw(seeds[4], (D // GROUP, FILT), FILT ** -0.5, 0.5, ((0, 4),))
    query_li = bell_draw(seeds[5], (WINDOW_SITES, D), 1.0, 6.0, ((0, 8), (1, 4)))
    key_li = bell_draw(seeds[6], (WINDOW_SITES, D), 1.0, 6.0, ((0, 8), (1, 4)))
    gain_li = jnp.clip(1.0 + 0.1 * jax.random.normal(seeds[7], (D,), jnp.float32), 0.5, 1.5)
    log_rates = draw_log_rates(jax.random.fold_in(seeds[12], 71), 0)
    retain = draw_retain(jax.random.fold_in(seeds[12], 71), 0)
    residues = bell_draw(seeds[10], (MODES, D), 0.25, 1.5, ((1, 4),), jnp.float32)
    cotangent = bell_draw(seeds[11], (WINDOW_SITES, D), 1.0, 6.0, ((0, 8), (1, 4)))
    return dict(tokens=tokens, query_mr=query_mr, key_mr=key_mr, gain_mr=gain_mr, filter_mr=filter_mr, query_li=query_li, key_li=key_li, gain_li=gain_li, log_rates=log_rates, retain=retain, residues=residues, cotangent=cotangent)


EPSILON = 1e-06

def rounded(value):
    narrow = lax.optimization_barrier(value.astype(jnp.bfloat16))
    return value + lax.stop_gradient(narrow.astype(jnp.float32) - value)

def rms_norm(values, gain):
    power = lax.optimization_barrier(jnp.mean(values * values, axis=1, keepdims=True))
    return values * gain[None, :] * lax.rsqrt(power + EPSILON)

def causal_groups(values, filters):
    groups, width = filters.shape
    row_ids = lax.broadcasted_iota(jnp.int32, (width, width), 0)
    column_indices = lax.broadcasted_iota(jnp.int32, (width, width), 1)
    lag_index = (row_ids - column_indices) % width
    table = jnp.take(filters, lag_index, axis=1)
    beneath_diagonal_strip = jnp.where(row_ids >= column_indices, table, jnp.zeros_like(table))
    upper_band = jnp.where(row_ids < column_indices, table, jnp.zeros_like(table))
    total, channels = values.shape
    padded = jnp.concatenate([jnp.zeros((width, channels), values.dtype), values], axis=0)
    blocks = padded.reshape(total // width + 1, width, groups, channels // groups)
    result = jnp.einsum('gij,bjgc->bigc', beneath_diagonal_strip, blocks[1:], precision=lax.Precision.HIGHEST)
    result = result + jnp.einsum('gij,bjgc->bigc', upper_band, blocks[:-1], precision=lax.Precision.HIGHEST)
    return result.reshape(total, channels)

def modal_filter(values, log_rates, retain, residues):
    rates = jnp.exp(log_rates)
    poles = jnp.exp(-rates)
    weight = residues * jnp.sqrt(-jnp.expm1(-2.0 * rates))
    total, channels = values.shape
    value_blocks = values.reshape(total // TOK_DEV, TOK_DEV, channels)
    retain_blocks = retain.reshape(total // TOK_DEV, TOK_DEV)

    def inner(carry, block):
        block_values, block_retain = block

        def advance(state, item):
            value_row, keep = item
            state = poles * keep * state + value_row[None, :]
            return (state, lax.optimization_barrier(jnp.sum(weight * state, axis=0)))
        return lax.scan(advance, carry, (block_values, block_retain))
    start = jnp.zeros(log_rates.shape, jnp.float32)
    final, outputs = lax.scan(jax.checkpoint(inner), start, (value_blocks, retain_blocks))
    return outputs.reshape(total, channels)

def forward(tokens, query_mr, key_mr, gain_mr, filter_mr, query_li, key_li, gain_li, log_rates, retain, residues):
    normed_in = rms_norm(tokens, gain_mr)
    mixed_in = rounded(key_mr * normed_in)
    conv_mr = causal_groups(mixed_in, filter_mr)
    middle = rounded(tokens + query_mr * conv_mr)
    normed_mid = rms_norm(middle, gain_li)
    conv_li = modal_filter(key_li * normed_mid, log_rates, retain, residues)
    return middle + query_li * conv_li

def reference(tokens, query_mr, key_mr, gain_mr, filter_mr, query_li, key_li, gain_li, log_rates, retain, residues, cotangent):
    inputs = (tokens, query_mr, key_mr, gain_mr, filter_mr, query_li, key_li, gain_li, log_rates, retain, residues)
    floats = tuple((item.astype(jnp.float32) for item in inputs))
    output, pullback = jax.vjp(forward, *floats)
    grads = pullback(cotangent.astype(jnp.float32))
    factor = lax.rsqrt(jnp.asarray(WINDOW_SITES, jnp.float32))
    return (output.astype(jnp.bfloat16), grads[0].astype(jnp.bfloat16), grads[1].astype(jnp.bfloat16), grads[2].astype(jnp.bfloat16), grads[5].astype(jnp.bfloat16), grads[6].astype(jnp.bfloat16), grads[3] * factor, grads[7] * factor, grads[4] * factor, grads[10] * factor, grads[8] * factor)
```

```python
import functools
import math

import jax
import jax.numpy as jnp
from jax import lax
from jax.experimental import pallas as pl
from jax.experimental.pallas import tpu as pltpu
from jax.sharding import PartitionSpec as P

EPSILON = 1e-06
LANES = 128
STEP = 16
F32 = jnp.float32
BF16 = jnp.bfloat16
MESH = pl.DeviceIdType.MESH


class Link:
    def __init__(self, sizes, send, recv):
        self.sizes, self.send, self.recv, self.used = sizes, send, recv, 0
        self.pending = []

    def greet(self, axes):
        barrier = pltpu.get_barrier_semaphore()
        greeted = 0
        for axis in axes:
            me = lax.axis_index(axis)
            for step in range(1, self.sizes[axis]):
                peer = lax.rem(me + step, self.sizes[axis])
                pl.semaphore_signal(barrier, inc=1, device_id={axis: peer}, device_id_type=MESH)
                greeted += 1
        return lambda: pl.semaphore_wait(barrier, greeted)

    def copy(self, source, target, axis, peer):
        slot = self.used
        self.used += 1
        return pltpu.make_async_remote_copy(
            src_ref=source,
            dst_ref=target,
            send_sem=self.send.at[slot],
            recv_sem=self.recv.at[slot],
            device_id={axis: peer},
            device_id_type=MESH,
        )

    def shift(self, source, target, axis, step):
        size = self.sizes[axis]
        me = lax.axis_index(axis)
        copy = self.copy(source, target, axis, lax.rem(me + step + size, size))
        sends = (me + step >= 0) & (me + step < size)
        gets = (me - step >= 0) & (me - step < size)
        pl.when(sends)(copy.start)
        self.pending.append(lambda: pl.when(sends)(copy.wait_send))
        return lambda: pl.when(gets)(copy.wait_recv)

    def gather(self, ref, axis):
        size = self.sizes[axis]
        me = lax.axis_index(axis)
        waits = []
        for step in range(1, size):
            copy = self.copy(ref.at[me], ref.at[me], axis, lax.rem(me + step, size))
            copy.start()
            self.pending.append(copy.wait_send)
            waits.append(copy.wait_recv)
        return lambda: [wait() for wait in waits]

    def scatter(self, source, piece, target, axis):
        size = self.sizes[axis]
        me = lax.axis_index(axis)
        waits = []
        for step in range(1, size):
            peer = lax.rem(me + step, size)
            rows = pl.ds(pl.multiple_of(peer * piece, STEP), piece)
            copy = self.copy(source.at[rows], target.at[me], axis, peer)
            copy.start()
            self.pending.append(copy.wait_send)
            waits.append(copy.wait_recv)
        return lambda: [wait() for wait in waits]

    def settle(self):
        for wait in self.pending:
            wait()


def hops(size):
    phases, cover = [[d for d in (1, 2) if d < size]], 2
    while cover < size:
        phases.append([cover * k for k in (1, 2, 3) if cover * k < size])
        cover *= 4
    return phases


def iota(shape, dim):
    return lax.broadcasted_iota(jnp.int32, shape, dim)


def dot(a, b):
    return jnp.dot(a, b, preferred_element_type=F32)


def column(row):
    return jnp.broadcast_to(row, (LANES, LANES)).T


def row8(partial):
    total = jnp.sum(partial, axis=1, keepdims=True)
    return jnp.broadcast_to(total, partial.shape).T[:8]


def lane_tile(j):
    if isinstance(j, int):
        return pl.ds(j * LANES, LANES)
    return pl.ds(pl.multiple_of(j * LANES, LANES), LANES)


def tree(terms):
    terms = list(terms)
    while len(terms) > 1:
        terms = [functools.reduce(lambda a, c: a + c, terms[k : k + 2]) for k in range(0, len(terms), 2)]
    return terms[0]


def windows(before, here):
    both = jnp.concatenate([before, here], axis=0)
    span = LANES + STEP
    return [both[k * STEP : k * STEP + span] for k in range(LANES // STEP)]


def band(row, back):
    table = pltpu.roll(
        jnp.broadcast_to(row, (STEP, LANES)), 0, 1, stride=1, stride_axis=0
    ).astype(BF16)
    r, c = iota((STEP, LANES), 0), iota((STEP, LANES), 1)
    zero = jnp.zeros_like(table)
    near = c >= r if back else c > r
    first = jnp.where(near, table, zero)
    second = jnp.where(near, zero, table)
    return jnp.concatenate([first, second[:, :STEP]], axis=1)


def filtered(taps, wins, back, owner):
    fold = taps.shape[0]
    left = jnp.concatenate([band(taps[g : g + 1], back) for g in range(fold)], axis=0)
    outs = dot(left, jnp.concatenate(wins, axis=1))
    blocks = []
    for k in range(len(wins)):
        at = slice(k * LANES, (k + 1) * LANES)
        block = outs[:STEP, at]
        for g in range(1, fold):
            block = jnp.where(owner == g, outs[g * STEP : (g + 1) * STEP, at], block)
        blocks.append(block)
    return jnp.concatenate(blocks, axis=0)


def tap_grads(turned, wins, owner, fold):
    count = len(wins)
    zero = jnp.zeros((STEP, LANES), BF16)
    left = jnp.concatenate(
        [
            jnp.concatenate(
                [
                    jnp.where(owner == g, turned[k * STEP : (k + 1) * STEP], zero)
                    for k in range(count)
                ],
                axis=1,
            )
            for g in range(fold)
        ],
        axis=0,
    )
    out = lax.dot_general(
        left, jnp.concatenate(wins, axis=1), (((1,), (1,)), ((), ())), preferred_element_type=F32
    )
    r, c = iota((STEP, LANES), 0), iota((STEP, LANES), 1)
    grads = []
    for g in range(fold):
        pair = out[g * STEP : (g + 1) * STEP]
        rest = jnp.concatenate([pair[:, LANES:], jnp.zeros((STEP, LANES - STEP), F32)], axis=1)
        pair = jnp.where(c > STEP - 1 - r, pair[:, :LANES], rest)
        pair = pltpu.roll(pair, 0, 1, stride=1, stride_axis=0)
        grads.append(jnp.sum(pair, axis=0, keepdims=True))
    return jnp.concatenate(grads, axis=0)


def decay_loss(rate):
    y = 2.0 * rate
    small = 1.0
    for k in range(8, 1, -1):
        small = 1.0 - y / k * small
    return jnp.where(y < 0.25, y * small, 1.0 - jnp.exp(-y))


INPUTS = (
    "x", "km", "gm", "cot", "ql", "keep", "lr", "res", "filt", "kl", "gl", "qm",
)
BIG = ("mixed", "gtok", "gqm", "gkm", "gql", "gkl")


def main_kernel(sizes, names, members, factor, *refs):
    ref = dict(zip(names, refs))
    hbm = {name: ref[name + "_in"] for name in INPUTS}
    ctx, tp = sizes["ctx"], sizes["tp"]
    rows, channels = ref["x"].shape
    modes = ref["lr"].shape[0]
    groups = ref["filt"].shape[0]
    tiles = channels // LANES
    width = channels * tp
    fold = LANES // members
    sub = min(8, tiles)
    bands = tiles // sub
    chunks = min(4, tiles)
    per = tiles // chunks
    span = channels // chunks
    pieces = [slice(c * span, (c + 1) * span) for c in range(chunks)]
    size = modes * tiles
    me_c = lax.axis_index("ctx")
    me_t = lax.axis_index("tp")
    owner = iota((STEP, LANES), 1) // members

    link = Link(sizes, ref["send"], ref["recv"])
    greeted = link.greet(["tp", "ctx"])
    loads = {}
    for k, name in enumerate(INPUTS):
        loads[name] = pltpu.make_async_copy(hbm[name], ref[name], ref["load"].at[k])
        loads[name].start()

    def need(*which):
        for name in which:
            loads[name].wait()

    stores = []

    def store(name):
        k = len(stores)
        copy = pltpu.make_async_copy(ref[name], ref[name + "_out"], ref["store"].at[k])
        copy.start()
        stores.append(copy)

    x_ref, km_ref, gm_ref = ref["x"], ref["km"], ref["gm"]
    early_ref, before_ref = ref["early"], ref["before"]

    need("x", "km", "gm")
    total = jnp.zeros((rows, LANES), F32)
    halo = []
    for c in range(chunks):
        def square(j, total):
            at = lane_tile(j)
            x = x_ref[:, at].astype(F32)
            early_ref[:, at] = (km_ref[:, at].astype(F32) * (x * gm_ref[:, at])).astype(BF16)
            return total + x * x

        total = lax.fori_loop(c * per, (c + 1) * per, square, total, unroll=per)
        if c == 0:
            greeted()
        halo.append(
            link.shift(early_ref.at[:, pieces[c]], before_ref.at[:, pieces[c]], "ctx", 1)
        )
    power_ref = ref["power"]
    power_ref[me_t] = row8(total)
    power_here = link.gather(power_ref, "tp")

    need("keep")
    lanes = iota((8, LANES), 1)
    run = jnp.broadcast_to(ref["keep"][...], (8, LANES))
    step = 1
    while step < LANES:
        run = run * jnp.where(lanes >= step, pltpu.roll(run, step, 1), 1.0)
        step *= 2
    share_ref = ref["share"]
    share_ref[me_c] = run
    share_here = link.gather(share_ref, "ctx")
    r_row = run[:1]
    r_col = column(r_row)
    r_end = jnp.broadcast_to(r_row[:, LANES - 1 :], (1, LANES))

    rate_ref, res_ref, pole_ref, weight_ref = ref["rate"], ref["resid"], ref["pole"], ref["weight"]
    need("lr", "res")
    for j in range(tiles):
        at = slice(j * LANES, (j + 1) * LANES)
        rate_ref[pl.ds(j, modes, stride=tiles), :] = jnp.exp(ref["lr"][:, at])
        res_ref[pl.ds(j, modes, stride=tiles), :] = ref["res"][:, at]
    pole_ref[...] = jnp.exp(-rate_ref[...])
    weight_ref[...] = res_ref[...] * jnp.sqrt(decay_loss(rate_ref[...]))

    g_ref, u_ref, y_ref, adj_ref = ref["g"], ref["u"], ref["y"], ref["adj"]
    need("cot", "ql")
    cot_ref, ql_ref = ref["cot"], ref["ql"]
    for j in range(tiles):
        at = slice(j * LANES, (j + 1) * LANES)
        g_ref[pl.ds(j, rows, stride=tiles), :] = (
            cot_ref[:, at].astype(F32) * ql_ref[:, at].astype(F32) * r_col
        )

    def places(b, first, count):
        return [pl.ds((first + n) * tiles + b * sub, sub) for n in range(count)]

    def at_time(t, b):
        return pl.ds(pl.multiple_of(t * tiles + b * sub, sub), sub)

    def sweep(source_ref, reverse, finish):
        for b in range(bands):
            where = places(b, 0, modes)
            pole = [pole_ref[at, :] for at in where]

            def advance(i, states, b=b, pole=pole):
                t = rows - 1 - i if reverse else i
                value = source_ref[at_time(t, b), :]
                return tuple(pole[n] * states[n] + value for n in range(modes))

            states = lax.fori_loop(
                0, rows, advance, tuple(jnp.zeros((sub, LANES), F32) for _ in range(modes)),
                unroll=4,
            )
            for n in range(modes):
                finish(where[n], pole[n], states[n])

    phases = hops(ctx)

    class Carry:
        def __init__(self, sign, send_refs, take_ref, total_ref):
            self.sign, self.send_refs, self.take_ref = sign, send_refs, take_ref
            self.total_ref, self.phase, self.slot = total_ref, 0, 0

        def launch(self):
            self.waits = []
            for distance in phases[self.phase]:
                wait = link.shift(
                    self.send_refs[self.phase], self.take_ref.at[self.slot], "ctx",
                    self.sign * distance,
                )
                self.waits.append((distance, self.slot, wait))
                self.slot += 1

        def share(self, count):
            out = jnp.ones((1, LANES), F32)
            for k in range(1, count + 1):
                who = jnp.clip(me_c - self.sign * k, 0, ctx - 1)
                out = out * jnp.broadcast_to(share_ref[who][:1, LANES - 1 :], (1, LANES))
            return out

        def collect(self):
            total = None if self.phase == 0 else self.total_ref[...]
            for distance, slot, wait in self.waits:
                wait()
                source = me_c - self.sign * distance
                live = (source >= 0) & (source < ctx)
                count = distance - 1 if self.phase == 0 else distance
                part = self.take_ref[slot].astype(F32)
                if count:
                    part = part * (jnp.exp(rate_ref[...] * float(-rows * count)) * self.share(count))
                part = jnp.where(live, part, 0.0)
                total = part if total is None else total + part
            self.total_ref[...] = total
            self.phase += 1
            if self.phase < len(phases):
                self.send_refs[self.phase][...] = total.astype(BF16)
                self.launch()

    lead = [ref[f"lead{k}"] for k in range(len(phases))]
    final = [ref[f"final{k}"] for k in range(len(phases))]

    def leave_lead(at, pole, state):
        lead[0][at, :] = (pole * state).astype(BF16)

    sweep(g_ref, True, leave_lead)
    later = Carry(-1, lead, ref["lead_all"], ref["ahead"])
    later.launch()

    need("filt")
    taps = ref["filt"][...]
    k0, k1 = iota((LANES, LANES), 0), iota((LANES, LANES), 1)
    mirror = jnp.where((k0 + k1) % LANES == 0, 1.0, 0.0).astype(BF16)
    ref["taps"][...] = taps.astype(F32)
    ref["flip"][...] = dot(taps, mirror)

    power_here()

    def gathered(of):
        out = of(0)
        for k in range(1, tp):
            out = out + of(k)
        return out

    sum_ref, sum_before_ref = ref["sum"], ref["sum_before"]
    sum_ref[...] = gathered(lambda k: power_ref[k])
    sum_here = link.shift(sum_ref, sum_before_ref, "ctx", 1)
    scale_in = column(lax.rsqrt(sum_ref[:1] / width + EPSILON))
    mix_ref = ref["mix"]

    def mix(j, _):
        at = lane_tile(j)
        normed = x_ref[:, at].astype(F32) * gm_ref[:, at] * scale_in
        mix_ref[:, at] = (km_ref[:, at].astype(F32) * normed).astype(BF16)
        return 0

    lax.fori_loop(0, tiles, mix, 0, unroll=per)

    @pl.when(me_c == 0)
    def _():
        before_ref[...] = jnp.zeros_like(before_ref)
        sum_before_ref[...] = jnp.zeros_like(sum_before_ref)

    sum_here()
    scale_before = column(lax.rsqrt(sum_before_ref[:1] / width + EPSILON))
    need("qm", "kl", "gl")
    qm_ref, kl_ref, gl_ref = ref["qm"], ref["kl"], ref["gl"]
    prev_ref, conv_ref, mid_ref = ref["prev"], ref["conv"], ref["mid"]

    def conv_tile(j, power):
        at = lane_tile(j)
        before = (before_ref[:, at].astype(F32) * scale_before).astype(BF16)
        prev_ref[:, at] = before
        taps = ref["flip"][pl.ds(pl.multiple_of(j * fold, fold), fold), :]
        conv = filtered(taps, windows(before, mix_ref[:, at]), False, owner)
        conv_ref[:, at] = conv
        mid = (x_ref[:, at].astype(F32) + qm_ref[:, at].astype(F32) * conv).astype(BF16)
        mid_ref[:, at] = mid
        mid = mid.astype(F32)
        return power + mid * mid

    def conv_chunk(c, power):
        halo[c]()
        return lax.fori_loop(c * per, (c + 1) * per, conv_tile, power, unroll=per)

    def adjoint():
        ahead_ref = ref["ahead"]
        for b in range(bands):
            where = places(b, 0, modes)
            pole = [pole_ref[at, :] for at in where]
            weight = [weight_ref[at, :] for at in where]

            def keep(t, adj, b=b, weight=weight):
                spot = (t * bands + b) * modes
                for n in range(modes):
                    adj_ref[spot + n] = adj[n]
                y_ref[at_time(t, b), :] = tree(weight[n] * adj[n] for n in range(modes))

            g = g_ref[at_time(rows - 1, b), :]
            start = tuple(ahead_ref[at, :] * r_end + g for at in where)
            keep(rows - 1, start)

            def back(i, adj, b=b, pole=pole, keep=keep):
                t = rows - 2 - i
                g = g_ref[at_time(t, b), :]
                adj = tuple(pole[n] * adj[n] + g for n in range(modes))
                keep(t, adj)
                return adj

            lax.fori_loop(0, rows - 1, back, start, unroll=2)

    share_here()
    power = jnp.zeros((rows, LANES), F32)
    for c in range(chunks):
        if c == chunks - 1:
            while later.phase < len(phases):
                later.collect()
            adjoint()
        power = conv_chunk(c, power)
        if c == 0:
            later.collect()

    inverse = 1.0 / r_col
    v_ref = ref["v"]
    total = jnp.zeros((rows, LANES), F32)
    for j in range(tiles):
        at = slice(j * LANES, (j + 1) * LANES)
        v = y_ref[pl.ds(j, rows, stride=tiles), :] * inverse
        v_ref[:, at] = v
        total = total + v * kl_ref[:, at].astype(F32) * gl_ref[:, at] * mid_ref[:, at].astype(F32)
    sums_ref = ref["sums"]
    sums_ref[me_t] = jnp.concatenate([row8(power), row8(total)], axis=0)
    link.gather(sums_ref, "tp")()
    power = gathered(lambda k: sums_ref[k])
    scale = column(lax.rsqrt(power[:1] / width + EPSILON))
    pull = scale * scale * scale * column(power[8:9]) / width

    gmid_ref, gconv_ref, next_ref = ref["gmid"], ref["gconv"], ref["next"]
    partf_ref = ref["partf"]
    gain_at = 2 * size + groups
    halo = []
    for c in range(chunks):
        for j in range(c * per, (c + 1) * per):
            at = slice(j * LANES, (j + 1) * LANES)
            mid = mid_ref[:, at].astype(F32)
            key = kl_ref[:, at].astype(F32)
            gain = gl_ref[:, at]
            v = v_ref[:, at]
            normed = mid * gain * scale
            ref["gkl"][:, at] = (v * normed).astype(BF16)
            u_ref[pl.ds(j, rows, stride=tiles), :] = key * normed * inverse
            grad = v * key * scale
            partf_ref[gain_at + tiles + j : gain_at + tiles + j + 1, :] = jnp.sum(
                grad * mid, axis=0, keepdims=True
            )
            gmid = cot_ref[:, at].astype(F32) + gain * grad - mid * pull
            gmid_ref[:, at] = gmid
            ref["gqm"][:, at] = (gmid * conv_ref[:, at]).astype(BF16)
            gconv_ref[:, at] = (gmid * qm_ref[:, at].astype(F32)).astype(BF16)
        halo.append(
            link.shift(gconv_ref.at[:, pieces[c]], next_ref.at[:, pieces[c]], "ctx", -1)
        )
    store("gkl")
    store("gqm")

    def leave_final(at, pole, state):
        final[0][at, :] = (state * r_end).astype(BF16)

    sweep(u_ref, False, leave_final)
    earlier = Carry(1, final, ref["final_all"], ref["behind"])
    earlier.launch()

    same = (k0 // STEP == k1 // STEP) & (k0 % STEP + k1 % STEP == STEP - 1)
    turn = jnp.where(same, 1.0, 0.0).astype(BF16)
    fgrad_ref = ref["fgrad"]

    def pair_tile(j, _):
        at = lane_tile(j)
        turned = dot(turn, gconv_ref[:, at]).astype(BF16)
        wins = windows(prev_ref[:, at], mix_ref[:, at])
        fgrad_ref[pl.ds(pl.multiple_of(j * fold, fold), fold), :] = tap_grads(
            turned, wins, owner, fold
        )
        return 0

    lax.fori_loop(0, tiles, pair_tile, 0, unroll=per)
    lag = jnp.where((k0 + k1) % LANES == STEP - 1, 1.0, 0.0).astype(BF16)
    partf_ref[2 * size : 2 * size + groups, :] = dot(fgrad_ref[...].astype(BF16), lag)
    earlier.collect()

    @pl.when(me_c == ctx - 1)
    def _():
        next_ref[...] = jnp.zeros_like(next_ref)

    gnorm_ref = ref["gnorm"]

    def back_tile(j, inner):
        at = lane_tile(j)
        taps = ref["taps"][pl.ds(pl.multiple_of(j * fold, fold), fold), :]
        wins = windows(gconv_ref[:, at], next_ref[:, at])
        gmix = filtered(taps, wins, True, owner)
        x = x_ref[:, at].astype(F32)
        gain = gm_ref[:, at]
        ref["gkm"][:, at] = (gmix * (x * gain * scale_in)).astype(BF16)
        gnorm = gmix * km_ref[:, at].astype(F32)
        gnorm_ref[:, at] = gnorm
        pulled = gnorm * x
        partf_ref[pl.ds(gain_at + j, 1), :] = jnp.sum(pulled * scale_in, axis=0, keepdims=True)
        return inner + pulled * gain

    def back_chunk(c, inner):
        halo[c]()
        return lax.fori_loop(c * per, (c + 1) * per, back_tile, inner, unroll=per)

    def forward():
        behind_ref = ref["behind"]
        half = min(8, modes)
        zero = jnp.zeros((sub, LANES), F32)
        for b in range(bands):
            for first in range(0, modes, half):
                where = places(b, first, half)
                pole = [pole_ref[at, :] for at in where]
                weight = [weight_ref[at, :] for at in where]

                def advance(t, carry, b=b, first=first, pole=pole, weight=weight):
                    at = at_time(t, b)
                    u = u_ref[at, :]
                    spot = (t * bands + b) * modes + first
                    states, wsum, psum = carry
                    adj = [adj_ref[spot + n] for n in range(half)]
                    psum = tuple(psum[n] + adj[n] * states[n] for n in range(half))
                    wsum = tuple(wsum[n] + adj[n] * u for n in range(half))
                    states = tuple(pole[n] * states[n] + u for n in range(half))
                    y = tree(weight[n] * states[n] for n in range(half))
                    y_ref[at, :] = y if first == 0 else y_ref[at, :] + y
                    return (states, wsum, psum)

                begin = tuple(behind_ref[at, :] for at in where)
                _, wsum, psum = lax.fori_loop(
                    0, rows, advance, (begin, (zero,) * half, (zero,) * half), unroll=2
                )
                for n in range(half):
                    at = where[n]
                    rate = rate_ref[at, :]
                    resid = res_ref[at, :]
                    spread = jnp.sqrt(decay_loss(rate))
                    slope = rate * resid * jnp.exp(-2.0 * rate) / spread
                    lean = rate * pole[n] * weight[n]
                    partf_ref[at, :] = spread * wsum[n]
                    partf_ref[pl.ds(size + at.start, sub), :] = slope * wsum[n] - lean * psum[n]

    inner = jnp.zeros((rows, LANES), F32)
    ahead = max(1, chunks // 2)
    for c in range(ahead):
        inner = back_chunk(c, inner)
    while earlier.phase < len(phases):
        earlier.collect()
    forward()
    for c in range(ahead, chunks):
        inner = back_chunk(c, inner)
    inner_ref = ref["inner"]
    inner_ref[me_t] = row8(inner)
    inner_here = link.gather(inner_ref, "tp")
    store("gkm")

    part_ref, pool_ref, sum_all_ref = ref["part"], ref["pool"], ref["totals_out"]
    piece = pool_ref.shape[1]
    used = gain_at + 2 * tiles
    if used < ctx * piece:
        partf_ref[used:, :] = jnp.zeros((ctx * piece - used, LANES), F32)
    part_ref[...] = partf_ref[...].astype(BF16)
    pool_here = link.scatter(part_ref, piece, pool_ref, "ctx")

    for j in range(tiles):
        at = slice(j * LANES, (j + 1) * LANES)
        conv = y_ref[pl.ds(j, rows, stride=tiles), :] * r_col
        ref["mixed"][:, at] = (
            mid_ref[:, at].astype(F32) + ql_ref[:, at].astype(F32) * conv
        ).astype(BF16)
        ref["gql"][:, at] = (cot_ref[:, at].astype(F32) * conv).astype(BF16)
    store("mixed")
    store("gql")

    pool_here()
    total = part_ref[pl.ds(pl.multiple_of(me_c * piece, STEP), piece), :].astype(F32)
    for step in range(1, ctx):
        total = total + pool_ref[lax.rem(me_c + step, ctx)].astype(F32)
    sum_all_ref[me_c] = (total * factor).astype(BF16)
    sum_all_here = link.gather(sum_all_ref, "ctx")

    inner_here()
    pull = scale_in * scale_in * scale_in * column(gathered(lambda k: inner_ref[k])[:1]) / width

    def last(j, _):
        at = lane_tile(j)
        ref["gtok"][:, at] = (
            gmid_ref[:, at]
            + gm_ref[:, at] * scale_in * gnorm_ref[:, at]
            - x_ref[:, at].astype(F32) * pull
        ).astype(BF16)
        return 0

    lax.fori_loop(0, tiles, last, 0, unroll=per)
    store("gtok")
    sum_all_here()
    link.settle()
    for copy in stores:
        copy.wait()


def finish_kernel(modes, groups, *refs):
    big, totals_ref = refs[: len(BIG)], refs[len(BIG)]
    outs = refs[len(BIG) + 1 : 2 * len(BIG) + 1]
    gain_mr_ref, gain_li_ref, filter_ref, res_ref, rate_ref, *held, flat_ref, come, go = refs[
        2 * len(BIG) + 1 :
    ]
    arrive = [
        pltpu.make_async_copy(source, hold, come.at[k])
        for k, (source, hold) in enumerate(zip(big, held))
    ]
    leave = [
        pltpu.make_async_copy(hold, target, go.at[k])
        for k, (hold, target) in enumerate(zip(held, outs))
    ]
    for copy in arrive:
        copy.start()
    for before, after in zip(arrive, leave):
        before.wait()
        after.start()
    tiles = gain_mr_ref.shape[0]
    size = modes * tiles
    flat_ref[...] = totals_ref[...].astype(F32)
    for j in range(tiles):
        at = slice(j * LANES, (j + 1) * LANES)
        res_ref[:, at] = flat_ref[pl.ds(j, modes, stride=tiles), :]
        rate_ref[:, at] = flat_ref[pl.ds(size + j, modes, stride=tiles), :]
    filter_ref[...] = flat_ref[2 * size : 2 * size + groups, :]
    gain_at = 2 * size + groups
    gain_mr_ref[...] = flat_ref[gain_at : gain_at + tiles, :]
    gain_li_ref[...] = flat_ref[gain_at + tiles : gain_at + 2 * tiles, :]
    for copy in leave:
        copy.wait()


def body(
    sizes,
    tokens,
    query_mr,
    key_mr,
    gain_mr,
    filter_mr,
    query_li,
    key_li,
    gain_li,
    log_rates,
    retain,
    residues,
    cotangent,
):
    rows, channels = tokens.shape
    groups, taps = filter_mr.shape
    members = channels // groups
    modes = log_rates.shape[0]
    tiles = channels // LANES
    ctx, tp = sizes["ctx"], sizes["tp"]
    factor = 1.0 / math.sqrt(rows * ctx)
    flat = (modes * tiles, LANES)
    full = (rows, channels)
    sub = min(8, tiles)
    chunks = min(4, tiles)

    given = dict(
        x=tokens, km=key_mr, gm=gain_mr[None, :], cot=cotangent, ql=query_li,
        keep=retain[None, :], lr=log_rates, res=residues, filt=filter_mr, kl=key_li,
        gl=gain_li[None, :], qm=query_mr,
    )
    height = 2 * modes * tiles + groups + 2 * tiles
    piece = -(-height // (STEP * ctx)) * STEP
    phases = hops(ctx)
    slots = sum(len(phase) for phase in phases)
    remote = 3 * (tp - 1) + 3 * (ctx - 1) + 2 * chunks + 1 + 2 * slots
    vmem = pltpu.VMEM
    dma = pltpu.SemaphoreType.DMA
    scratch = {name: vmem(given[name].shape, given[name].dtype) for name in INPUTS}
    scratch |= {name: vmem(full, BF16) for name in BIG}
    scratch |= {
        name: vmem(full, BF16)
        for name in ("early", "before", "mix", "prev", "mid", "gconv", "next")
    }
    scratch |= {name: vmem(full, F32) for name in ("conv", "v", "gmid", "gnorm")}
    scratch |= {name: vmem((rows * tiles, LANES), F32) for name in ("g", "u", "y")}
    scratch["adj"] = vmem((rows * (tiles // sub) * modes, sub, LANES), F32)
    scratch |= {
        name: vmem(flat, F32) for name in ("rate", "resid", "pole", "weight", "ahead", "behind")
    }
    for k in range(len(phases)):
        scratch |= {f"lead{k}": vmem(flat, BF16), f"final{k}": vmem(flat, BF16)}
    scratch |= {name: vmem((slots,) + flat, BF16) for name in ("lead_all", "final_all")}
    scratch |= {
        "power": vmem((tp, 8, rows), F32),
        "share": vmem((ctx, 8, rows), F32),
        "sum": vmem((8, rows), F32),
        "sum_before": vmem((8, rows), F32),
        "sums": vmem((tp, 16, rows), F32),
        "inner": vmem((tp, 8, rows), F32),
        "taps": vmem((groups, taps), F32),
        "flip": vmem((groups, taps), F32),
        "fgrad": vmem((groups, taps), F32),
        "partf": vmem((ctx * piece, LANES), F32),
        "part": vmem((ctx * piece, LANES), BF16),
        "pool": vmem((ctx, piece, LANES), BF16),
        "send": dma((remote,)),
        "recv": dma((remote,)),
        "load": dma((len(INPUTS),)),
        "store": dma((len(BIG),)),
    }
    names = (
        [name + "_in" for name in INPUTS]
        + [name + "_out" for name in BIG]
        + ["totals_out"]
        + list(scratch)
    )
    anywhere = pl.BlockSpec(memory_space=pl.ANY)
    inside = pl.BlockSpec(memory_space=pltpu.VMEM)
    *big, totals = pl.pallas_call(
        functools.partial(main_kernel, sizes, names, members, factor),
        name="pair",
        out_shape=[jax.ShapeDtypeStruct(full, BF16) for _ in BIG]
        + [jax.ShapeDtypeStruct((ctx, piece, LANES), BF16)],
        in_specs=[anywhere] * len(INPUTS),
        out_specs=[anywhere] * len(BIG) + [inside],
        scratch_shapes=list(scratch.values()),
        compiler_params=pltpu.CompilerParams(
            collective_id=1, has_side_effects=True, vmem_limit_bytes=56 * 2**20
        ),
    )(*[given[name] for name in INPUTS])
    outs = [(full, BF16)] * len(BIG) + [
        ((tiles, LANES), F32), ((tiles, LANES), F32), ((groups, taps), F32),
        ((modes, channels), F32), ((modes, channels), F32),
    ]
    mixed, gtok, gqm, gkm, gql, gkl, ggm, ggl, gfilt, gres, grate = pl.pallas_call(
        functools.partial(finish_kernel, modes, groups),
        name="results",
        out_shape=[jax.ShapeDtypeStruct(s, d) for s, d in outs],
        in_specs=[anywhere] * len(BIG) + [inside],
        out_specs=[anywhere] * len(BIG) + [inside] * 5,
        scratch_shapes=[vmem(full, BF16)] * len(BIG)
        + [vmem((ctx * piece, LANES), F32), dma((len(BIG),)), dma((len(BIG),))],
    )(*big, totals.reshape(ctx * piece, LANES))
    return (
        mixed, gtok, gqm, gkm, gql, gkl, ggm.reshape(channels), ggl.reshape(channels),
        gfilt, gres, grate,
    )


def solution(mesh):
    wide, tall, both = P("tp"), P("tp", None), P("ctx", "tp")
    across = P(None, "tp")
    return jax.shard_map(
        functools.partial(body, dict(mesh.shape)),
        mesh=mesh,
        in_specs=(
            both, both, both, wide, tall, both, both, wide, across, P("ctx"), across, both,
        ),
        out_specs=(both,) * 6 + (wide, wide, tall, across, across),
        check_vma=False,
    )
```

```python
import functools
import math

import jax
import jax.numpy as jnp
from jax import lax
from jax.experimental import pallas as pl
from jax.experimental.pallas import tpu as pltpu
from jax.sharding import PartitionSpec as P

EPSILON = 1e-06
LANES = 128
STEP = 16
POOL_LATE = True
MEET_FIRST = True
EARLY = 0
CUT = (2, 1, 1, 0)
F32 = jnp.float32
BF16 = jnp.bfloat16
MESH = pl.DeviceIdType.MESH


class Link:
    def __init__(self, sizes, send, recv):
        self.sizes, self.send, self.recv, self.used = sizes, send, recv, 0
        self.pending = []

    def greet(self, axes):
        barrier = pltpu.get_barrier_semaphore()
        greeted = 0
        for axis in axes:
            me = lax.axis_index(axis)
            for step in range(1, self.sizes[axis]):
                peer = lax.rem(me + step, self.sizes[axis])
                pl.semaphore_signal(barrier, inc=1, device_id={axis: peer}, device_id_type=MESH)
                greeted += 1
        return lambda: pl.semaphore_wait(barrier, greeted)

    def copy(self, source, target, axis, peer):
        slot = self.used
        self.used += 1
        return pltpu.make_async_remote_copy(
            src_ref=source,
            dst_ref=target,
            send_sem=self.send.at[slot],
            recv_sem=self.recv.at[slot],
            device_id={axis: peer},
            device_id_type=MESH,
        )

    def shift(self, source, target, axis, step):
        size = self.sizes[axis]
        me = lax.axis_index(axis)
        copy = self.copy(source, target, axis, lax.rem(me + step + size, size))
        sends = (me + step >= 0) & (me + step < size)
        gets = (me - step >= 0) & (me - step < size)
        pl.when(sends)(copy.start)
        self.pending.append(lambda: pl.when(sends)(copy.wait_send))
        return lambda: pl.when(gets)(copy.wait_recv)

    def gather(self, ref, axis):
        size = self.sizes[axis]
        me = lax.axis_index(axis)
        waits = []
        for step in range(1, size):
            copy = self.copy(ref.at[me], ref.at[me], axis, lax.rem(me + step, size))
            copy.start()
            self.pending.append(copy.wait_send)
            waits.append(copy.wait_recv)
        return lambda: [wait() for wait in waits]

    def scatter(self, source, piece, target, axis):
        size = self.sizes[axis]
        me = lax.axis_index(axis)
        waits = []
        for step in range(1, size):
            peer = lax.rem(me + step, size)
            rows = pl.ds(pl.multiple_of(peer * piece, STEP), piece)
            copy = self.copy(source.at[rows], target.at[me], axis, peer)
            copy.start()
            self.pending.append(copy.wait_send)
            waits.append(copy.wait_recv)
        return lambda: [wait() for wait in waits]

    def settle(self):
        for wait in self.pending:
            wait()


def hops(size):
    phases, cover = [[d for d in (1, 2) if d < size]], 2
    while cover < size:
        phases.append([cover * k for k in (1, 2, 3) if cover * k < size])
        cover *= 4
    return phases


def iota(shape, dim):
    return lax.broadcasted_iota(jnp.int32, shape, dim)


def dot(a, b):
    return jnp.dot(a, b, preferred_element_type=F32)


def column(row):
    return jnp.broadcast_to(row, (LANES, LANES)).T


def row8(partial):
    total = jnp.sum(partial, axis=1, keepdims=True)
    return jnp.broadcast_to(total, partial.shape).T[:8]


def lane_tile(j):
    if isinstance(j, int):
        return pl.ds(j * LANES, LANES)
    return pl.ds(pl.multiple_of(j * LANES, LANES), LANES)


def tree(terms):
    terms = list(terms)
    while len(terms) > 1:
        terms = [functools.reduce(lambda a, c: a + c, terms[k : k + 2]) for k in range(0, len(terms), 2)]
    return terms[0]


def windows(before, here):
    both = jnp.concatenate([before, here], axis=0)
    span = LANES + STEP
    return [both[k * STEP : k * STEP + span] for k in range(LANES // STEP)]


def band(row, back):
    table = pltpu.roll(
        jnp.broadcast_to(row, (STEP, LANES)), 0, 1, stride=1, stride_axis=0
    ).astype(BF16)
    r, c = iota((STEP, LANES), 0), iota((STEP, LANES), 1)
    zero = jnp.zeros_like(table)
    near = c >= r if back else c > r
    first = jnp.where(near, table, zero)
    second = jnp.where(near, zero, table)
    return jnp.concatenate([first, second[:, :STEP]], axis=1)


def filtered(taps, wins, back, owner):
    fold = taps.shape[0]
    left = jnp.concatenate([band(taps[g : g + 1], back) for g in range(fold)], axis=0)
    outs = dot(left, jnp.concatenate(wins, axis=1))
    blocks = []
    for k in range(len(wins)):
        at = slice(k * LANES, (k + 1) * LANES)
        block = outs[:STEP, at]
        for g in range(1, fold):
            block = jnp.where(owner == g, outs[g * STEP : (g + 1) * STEP, at], block)
        blocks.append(block)
    return jnp.concatenate(blocks, axis=0)


def tap_grads(turned, wins, owner, fold):
    count = len(wins)
    zero = jnp.zeros((STEP, LANES), BF16)
    left = jnp.concatenate(
        [
            jnp.concatenate(
                [
                    jnp.where(owner == g, turned[k * STEP : (k + 1) * STEP], zero)
                    for k in range(count)
                ],
                axis=1,
            )
            for g in range(fold)
        ],
        axis=0,
    )
    out = lax.dot_general(
        left, jnp.concatenate(wins, axis=1), (((1,), (1,)), ((), ())), preferred_element_type=F32
    )
    r, c = iota((STEP, LANES), 0), iota((STEP, LANES), 1)
    grads = []
    for g in range(fold):
        pair = out[g * STEP : (g + 1) * STEP]
        rest = jnp.concatenate([pair[:, LANES:], jnp.zeros((STEP, LANES - STEP), F32)], axis=1)
        pair = jnp.where(c > STEP - 1 - r, pair[:, :LANES], rest)
        pair = pltpu.roll(pair, 0, 1, stride=1, stride_axis=0)
        grads.append(jnp.sum(pair, axis=0, keepdims=True))
    return jnp.concatenate(grads, axis=0)


def decay_loss(rate):
    y = 2.0 * rate
    small = 1.0
    for k in range(8, 1, -1):
        small = 1.0 - y / k * small
    return jnp.where(y < 0.25, y * small, 1.0 - jnp.exp(-y))


INPUTS = (
    "lr", "res", "keep", "cot", "ql", "x", "km", "gm", "filt", "qm", "kl", "gl",
)
BIG = ("mixed", "gtok", "gqm", "gkm", "gql", "gkl")


def main_kernel(sizes, names, members, factor, *refs):
    ref = dict(zip(names, refs))
    hbm = {name: ref[name + "_in"] for name in INPUTS}
    ctx, tp = sizes["ctx"], sizes["tp"]
    rows, channels = ref["x"].shape
    modes = ref["lr"].shape[0]
    groups = ref["filt"].shape[0]
    tiles = channels // LANES
    width = channels * tp
    fold = LANES // members
    sub = min(8, tiles)
    bands = tiles // sub
    chunks = min(4, tiles)
    per = tiles // chunks
    span = channels // chunks
    pieces = [slice(c * span, (c + 1) * span) for c in range(chunks)]
    size = modes * tiles
    me_c = lax.axis_index("ctx")
    me_t = lax.axis_index("tp")
    owner = iota((STEP, LANES), 1) // members

    link = Link(sizes, ref["send"], ref["recv"])
    greeted = link.greet(["tp", "ctx"])
    loads = {}
    for k, name in enumerate(INPUTS):
        loads[name] = pltpu.make_async_copy(hbm[name], ref[name], ref["load"].at[k])
        loads[name].start()

    def need(*which):
        for name in which:
            loads[name].wait()

    stores = []

    def store(name):
        k = len(stores)
        copy = pltpu.make_async_copy(ref[name], ref[name + "_out"], ref["store"].at[k])
        copy.start()
        stores.append(copy)

    x_ref, km_ref, gm_ref = ref["x"], ref["km"], ref["gm"]
    early_ref, before_ref = ref["early"], ref["before"]

    need("keep")
    lanes = iota((8, LANES), 1)
    run = jnp.broadcast_to(ref["keep"][...], (8, LANES))
    step = 1
    while step < LANES:
        run = run * jnp.where(lanes >= step, pltpu.roll(run, step, 1), 1.0)
        step *= 2
    share_ref = ref["share"]
    share_ref[me_c] = run
    greeted()
    share_here = link.gather(share_ref, "ctx")
    r_row = run[:1]
    r_col = column(r_row)
    r_end = jnp.broadcast_to(r_row[:, LANES - 1 :], (1, LANES))

    rate_ref, res_ref, pole_ref, weight_ref = ref["rate"], ref["resid"], ref["pole"], ref["weight"]
    need("lr", "res")
    for j in range(tiles):
        at = slice(j * LANES, (j + 1) * LANES)
        rate_ref[pl.ds(j, modes, stride=tiles), :] = jnp.exp(ref["lr"][:, at])
        res_ref[pl.ds(j, modes, stride=tiles), :] = ref["res"][:, at]
    pole_ref[...] = jnp.exp(-rate_ref[...])
    weight_ref[...] = res_ref[...] * jnp.sqrt(decay_loss(rate_ref[...]))

    g_ref, u_ref, y_ref, adj_ref = ref["g"], ref["u"], ref["y"], ref["adj"]
    need("cot", "ql")
    cot_ref, ql_ref = ref["cot"], ref["ql"]
    for j in range(tiles):
        at = slice(j * LANES, (j + 1) * LANES)
        g_ref[pl.ds(j, rows, stride=tiles), :] = (
            cot_ref[:, at].astype(F32) * ql_ref[:, at].astype(F32) * r_col
        )

    def places(b, first, count):
        return [pl.ds((first + n) * tiles + b * sub, sub) for n in range(count)]

    def at_time(t, b):
        return pl.ds(pl.multiple_of(t * tiles + b * sub, sub), sub)

    def sweep(source_ref, reverse, finish):
        for b in range(bands):
            where = places(b, 0, modes)
            pole = [pole_ref[at, :] for at in where]

            def advance(i, states, b=b, pole=pole):
                t = rows - 1 - i if reverse else i
                value = source_ref[at_time(t, b), :]
                return tuple(pole[n] * states[n] + value for n in range(modes))

            states = lax.fori_loop(
                0, rows, advance, tuple(jnp.zeros((sub, LANES), F32) for _ in range(modes)),
                unroll=4,
            )
            for n in range(modes):
                finish(where[n], pole[n], states[n])

    phases = hops(ctx)

    class Carry:
        def __init__(self, sign, send_refs, take_ref, total_ref):
            self.sign, self.send_refs, self.take_ref = sign, send_refs, take_ref
            self.total_ref, self.phase, self.slot = total_ref, 0, 0

        def launch(self):
            self.waits = []
            for distance in phases[self.phase]:
                wait = link.shift(
                    self.send_refs[self.phase], self.take_ref.at[self.slot], "ctx",
                    self.sign * distance,
                )
                self.waits.append((distance, self.slot, wait))
                self.slot += 1

        def share(self, count):
            out = jnp.ones((1, LANES), F32)
            for k in range(1, count + 1):
                who = jnp.clip(me_c - self.sign * k, 0, ctx - 1)
                out = out * jnp.broadcast_to(share_ref[who][:1, LANES - 1 :], (1, LANES))
            return out

        def collect(self):
            total = None if self.phase == 0 else self.total_ref[...]
            for distance, slot, wait in self.waits:
                wait()
                source = me_c - self.sign * distance
                live = (source >= 0) & (source < ctx)
                count = distance - 1 if self.phase == 0 else distance
                part = self.take_ref[slot].astype(F32)
                if count:
                    part = part * (jnp.exp(rate_ref[...] * float(-rows * count)) * self.share(count))
                part = jnp.where(live, part, 0.0)
                total = part if total is None else total + part
            self.total_ref[...] = total
            self.phase += 1
            if self.phase < len(phases):
                self.send_refs[self.phase][...] = total.astype(BF16)
                self.launch()

    lead = [ref[f"lead{k}"] for k in range(len(phases))]
    final = [ref[f"final{k}"] for k in range(len(phases))]

    def leave_lead(at, pole, state):
        lead[0][at, :] = (pole * state).astype(BF16)

    sweep(g_ref, True, leave_lead)
    later = Carry(-1, lead, ref["lead_all"], ref["ahead"])
    later.launch()

    need("x", "km", "gm")
    total = jnp.zeros((rows, LANES), F32)
    halo = []

    def ahead_chunk(c):
        halo.append(
            link.shift(early_ref.at[:, pieces[c]], before_ref.at[:, pieces[c]], "ctx", 1)
        )

    for c in range(chunks):
        def square(j, total):
            at = lane_tile(j)
            x = x_ref[:, at].astype(F32)
            early_ref[:, at] = (km_ref[:, at].astype(F32) * (x * gm_ref[:, at])).astype(BF16)
            return total + x * x

        total = lax.fori_loop(c * per, (c + 1) * per, square, total, unroll=per)
    cut = [chunks * k // 4 for k in CUT]
    for c in range(cut[0]):
        ahead_chunk(c)
    power_ref = ref["power"]
    power_ref[me_t] = row8(total)
    power_here = link.gather(power_ref, "tp")

    need("filt")
    taps = ref["filt"][...]
    k0, k1 = iota((LANES, LANES), 0), iota((LANES, LANES), 1)
    mirror = jnp.where((k0 + k1) % LANES == 0, 1.0, 0.0).astype(BF16)
    ref["taps"][...] = taps.astype(F32)
    ref["flip"][...] = dot(taps, mirror)

    power_here()

    def gathered(of):
        out = of(0)
        for k in range(1, tp):
            out = out + of(k)
        return out

    sum_ref, sum_before_ref = ref["sum"], ref["sum_before"]
    sum_ref[...] = gathered(lambda k: power_ref[k])
    sum_here = link.shift(sum_ref, sum_before_ref, "ctx", 1)
    scale_in = column(lax.rsqrt(sum_ref[:1] / width + EPSILON))
    mix_ref = ref["mix"]

    def mix(j, _):
        at = lane_tile(j)
        normed = x_ref[:, at].astype(F32) * gm_ref[:, at] * scale_in
        mix_ref[:, at] = (km_ref[:, at].astype(F32) * normed).astype(BF16)
        return 0

    lax.fori_loop(0, tiles, mix, 0, unroll=per)

    @pl.when(me_c == 0)
    def _():
        before_ref[...] = jnp.zeros_like(before_ref)
        sum_before_ref[...] = jnp.zeros_like(sum_before_ref)

    sum_here()
    scale_before = column(lax.rsqrt(sum_before_ref[:1] / width + EPSILON))
    need("qm", "kl", "gl")
    qm_ref, kl_ref, gl_ref = ref["qm"], ref["kl"], ref["gl"]
    prev_ref, conv_ref, mid_ref = ref["prev"], ref["conv"], ref["mid"]

    def conv_tile(j, power):
        at = lane_tile(j)
        before = (before_ref[:, at].astype(F32) * scale_before).astype(BF16)
        prev_ref[:, at] = before
        taps = ref["flip"][pl.ds(pl.multiple_of(j * fold, fold), fold), :]
        conv = filtered(taps, windows(before, mix_ref[:, at]), False, owner)
        conv_ref[:, at] = conv
        mid = (x_ref[:, at].astype(F32) + qm_ref[:, at].astype(F32) * conv).astype(BF16)
        mid_ref[:, at] = mid
        mid = mid.astype(F32)
        return power + mid * mid

    def conv_chunk(c, power):
        halo[c]()
        return lax.fori_loop(c * per, (c + 1) * per, conv_tile, power, unroll=per)

    def adjoint():
        ahead_ref = ref["ahead"]
        for b in range(bands):
            where = places(b, 0, modes)
            pole = [pole_ref[at, :] for at in where]
            weight = [weight_ref[at, :] for at in where]

            def keep(t, adj, b=b, weight=weight):
                spot = (t * bands + b) * modes
                for n in range(modes):
                    adj_ref[spot + n] = adj[n]
                y_ref[at_time(t, b), :] = tree(weight[n] * adj[n] for n in range(modes))

            g = g_ref[at_time(rows - 1, b), :]
            start = tuple(ahead_ref[at, :] * r_end + g for at in where)
            keep(rows - 1, start)

            def back(i, adj, b=b, pole=pole, keep=keep):
                t = rows - 2 - i
                g = g_ref[at_time(t, b), :]
                adj = tuple(pole[n] * adj[n] + g for n in range(modes))
                keep(t, adj)
                return adj

            lax.fori_loop(0, rows - 1, back, start, unroll=2)

    inverse = 1.0 / r_col
    v_ref = ref["v"]

    def pulled(c, total):
        for j in range(c * per, (c + 1) * per):
            at = slice(j * LANES, (j + 1) * LANES)
            v = y_ref[pl.ds(j, rows, stride=tiles), :] * inverse
            v_ref[:, at] = v
            here = v * kl_ref[:, at].astype(F32) * gl_ref[:, at] * mid_ref[:, at].astype(F32)
            total = total + here
        return total

    share_here()
    power = jnp.zeros((rows, LANES), F32)
    total = jnp.zeros((rows, LANES), F32)
    later.collect()
    for c in range(cut[0], chunks):
        ahead_chunk(c)
    for c in range(chunks):
        if c == chunks - 1:
            while later.phase < len(phases):
                later.collect()
            adjoint()
            for done in range(c):
                total = pulled(done, total)
        power = conv_chunk(c, power)
    total = pulled(chunks - 1, total)
    sums_ref = ref["sums"]
    sums_ref[me_t] = jnp.concatenate([row8(power), row8(total)], axis=0)
    link.gather(sums_ref, "tp")()
    power = gathered(lambda k: sums_ref[k])
    scale = column(lax.rsqrt(power[:1] / width + EPSILON))
    pull = scale * scale * scale * column(power[8:9]) / width

    gmid_ref, gconv_ref, next_ref = ref["gmid"], ref["gconv"], ref["next"]
    partf_ref = ref["partf"]
    bend_ref = ref["bend"]
    halo = []

    def leave_final(at, pole, state):
        final[0][at, :] = (state * r_end).astype(BF16)

    earlier = Carry(1, final, ref["final_all"], ref["behind"])

    def normed_tile(j):
        at = slice(j * LANES, (j + 1) * LANES)
        normed = mid_ref[:, at].astype(F32) * gl_ref[:, at] * scale
        u_ref[pl.ds(j, rows, stride=tiles), :] = kl_ref[:, at].astype(F32) * normed * inverse
        ref["gkl"][:, at] = (v_ref[:, at] * normed).astype(BF16)

    def behind_chunk(c):
        halo.append(
            link.shift(gconv_ref.at[:, pieces[c]], next_ref.at[:, pieces[c]], "ctx", -1)
        )

    for j in range(tiles):
        if j == cut[1] * per:
            for k in range(tiles):
                normed_tile(k)
            sweep(u_ref, False, leave_final)
            earlier.launch()
        at = slice(j * LANES, (j + 1) * LANES)
        mid = mid_ref[:, at].astype(F32)
        gain = gl_ref[:, at]
        grad = v_ref[:, at] * kl_ref[:, at].astype(F32) * scale
        bend_ref[tiles + j : tiles + j + 1, :] = jnp.sum(grad * mid, axis=0, keepdims=True)
        gmid = cot_ref[:, at].astype(F32) + gain * grad - mid * pull
        gmid_ref[:, at] = gmid
        ref["gqm"][:, at] = (gmid * conv_ref[:, at]).astype(BF16)
        gconv_ref[:, at] = (gmid * qm_ref[:, at].astype(F32)).astype(BF16)
        if j % per == per - 1 and j // per < cut[2]:
            behind_chunk(j // per)
    store("gkl")
    store("gqm")

    half = min(8, modes)
    zero = jnp.zeros((sub, LANES), F32)
    wsum_ref = ref["wsum"]
    def meet_all():
        for b in range(bands):
            def meet(t, sums, b=b):
                u = u_ref[at_time(t, b), :]
                spot = (t * bands + b) * modes
                return tuple(sums[n] + adj_ref[spot + n] * u for n in range(modes))

            sums = lax.fori_loop(0, rows, meet, (zero,) * modes, unroll=4)
            for n, at in enumerate(places(b, 0, modes)):
                wsum_ref[at, :] = sums[n]
    if MEET_FIRST:
        meet_all()
    earlier.collect()
    for c in range(cut[2], chunks):
        behind_chunk(c)
    if not MEET_FIRST:
        meet_all()

    same = (k0 // STEP == k1 // STEP) & (k0 % STEP + k1 % STEP == STEP - 1)
    turn = jnp.where(same, 1.0, 0.0).astype(BF16)
    fgrad_ref = ref["fgrad"]

    def pair_tile(j, _):
        at = lane_tile(j)
        turned = dot(turn, gconv_ref[:, at]).astype(BF16)
        wins = windows(prev_ref[:, at], mix_ref[:, at])
        fgrad_ref[pl.ds(pl.multiple_of(j * fold, fold), fold), :] = tap_grads(
            turned, wins, owner, fold
        )
        return 0

    lax.fori_loop(0, tiles, pair_tile, 0, unroll=per)
    lag = jnp.where((k0 + k1) % LANES == STEP - 1, 1.0, 0.0).astype(BF16)
    tap_part_ref, tap_pool_ref, tap_all_ref = ref["tap_part"], ref["tap_pool"], ref["taps_out"]
    share_rows = tap_pool_ref.shape[1]
    turned_back = dot(fgrad_ref[...].astype(BF16), lag).astype(BF16)
    if groups < ctx * share_rows:
        tap_part_ref[groups:, :] = jnp.zeros((ctx * share_rows - groups, LANES), BF16)
    tap_part_ref[:groups, :] = turned_back
    tap_here = link.scatter(tap_part_ref, share_rows, tap_pool_ref, "ctx")

    @pl.when(me_c == ctx - 1)
    def _():
        next_ref[...] = jnp.zeros_like(next_ref)

    gnorm_ref = ref["gnorm"]
    def back_tile(j, inner):
        at = lane_tile(j)
        taps = ref["taps"][pl.ds(pl.multiple_of(j * fold, fold), fold), :]
        wins = windows(gconv_ref[:, at], next_ref[:, at])
        gmix = filtered(taps, wins, True, owner)
        x = x_ref[:, at].astype(F32)
        gain = gm_ref[:, at]
        ref["gkm"][:, at] = (gmix * (x * gain * scale_in)).astype(BF16)
        gnorm = gmix * km_ref[:, at].astype(F32)
        gnorm_ref[:, at] = gnorm
        drawn = gnorm * x
        bend_ref[pl.ds(j, 1), :] = jnp.sum(drawn * scale_in, axis=0, keepdims=True)
        return inner + drawn * gain

    def back_chunk(c, inner):
        halo[c]()
        return lax.fori_loop(c * per, (c + 1) * per, back_tile, inner, unroll=per)

    def forward():
        behind_ref = ref["behind"]
        for b in range(bands):
            for first in range(0, modes, half):
                where = places(b, first, half)
                pole = [pole_ref[at, :] for at in where]
                weight = [weight_ref[at, :] for at in where]

                def advance(t, carry, b=b, first=first, pole=pole, weight=weight):
                    at = at_time(t, b)
                    u = u_ref[at, :]
                    spot = (t * bands + b) * modes + first
                    states, psum = carry
                    adj = [adj_ref[spot + n] for n in range(half)]
                    psum = tuple(psum[n] + adj[n] * states[n] for n in range(half))
                    states = tuple(pole[n] * states[n] + u for n in range(half))
                    y = tree(weight[n] * states[n] for n in range(half))
                    y_ref[at, :] = y if first == 0 else y_ref[at, :] + y
                    return (states, psum)

                begin = tuple(behind_ref[at, :] for at in where)
                _, psum = lax.fori_loop(0, rows, advance, (begin, (zero,) * half), unroll=2)
                for n in range(half):
                    at = where[n]
                    rate = rate_ref[at, :]
                    resid = res_ref[at, :]
                    spread = jnp.sqrt(decay_loss(rate))
                    slope = rate * resid * jnp.exp(-2.0 * rate) / spread
                    lean = rate * pole[n] * weight[n]
                    wsum = wsum_ref[at, :]
                    partf_ref[at, :] = spread * wsum
                    partf_ref[pl.ds(size + at.start, sub), :] = slope * wsum - lean * psum[n]

    inner = jnp.zeros((rows, LANES), F32)
    early = min(EARLY, chunks - 1)
    for c in range(early):
        inner = back_chunk(c, inner)
    while earlier.phase < len(phases):
        earlier.collect()
    forward()

    part_ref, pool_ref, sum_all_ref = ref["part"], ref["pool"], ref["totals_out"]
    piece = pool_ref.shape[1]
    used = 2 * size
    if used < ctx * piece:
        partf_ref[used:, :] = jnp.zeros((ctx * piece - used, LANES), F32)
    part_ref[...] = partf_ref[...].astype(BF16)
    if cut[3] == 0:
        pool_here = link.scatter(part_ref, piece, pool_ref, "ctx")

    def summed(part_ref, pool_ref, all_ref):
        count = pool_ref.shape[1]
        total = part_ref[pl.ds(pl.multiple_of(me_c * count, STEP), count), :].astype(F32)
        for step in range(1, ctx):
            total = total + pool_ref[lax.rem(me_c + step, ctx)].astype(F32)
        all_ref[me_c] = (total * factor).astype(BF16)
        return link.gather(all_ref, "ctx")

    for c in range(early, chunks):
        inner = back_chunk(c, inner)
        if c + 1 == cut[3]:
            pool_here = link.scatter(part_ref, piece, pool_ref, "ctx")
    inner_ref = ref["inner"]
    inner_ref[me_t] = row8(inner)
    inner_here = link.gather(inner_ref, "tp")
    bends_ref = ref["bends"]
    bends_ref[me_c] = bend_ref[...]
    bends_here = link.gather(bends_ref, "ctx")
    store("gkm")

    tap_here()
    tap_all_here = summed(tap_part_ref, tap_pool_ref, tap_all_ref)
    if not POOL_LATE:
        pool_here()
        sum_all_here = summed(part_ref, pool_ref, sum_all_ref)
    for j in range(tiles):
        at = slice(j * LANES, (j + 1) * LANES)
        conv = y_ref[pl.ds(j, rows, stride=tiles), :] * r_col
        ref["mixed"][:, at] = (
            mid_ref[:, at].astype(F32) + ql_ref[:, at].astype(F32) * conv
        ).astype(BF16)
        ref["gql"][:, at] = (cot_ref[:, at].astype(F32) * conv).astype(BF16)
    store("mixed")
    store("gql")

    if POOL_LATE:
        pool_here()
        sum_all_here = summed(part_ref, pool_ref, sum_all_ref)
    inner_here()
    pull = scale_in * scale_in * scale_in * column(gathered(lambda k: inner_ref[k])[:1]) / width

    def last(j, _):
        at = lane_tile(j)
        ref["gtok"][:, at] = (
            gmid_ref[:, at]
            + gm_ref[:, at] * scale_in * gnorm_ref[:, at]
            - x_ref[:, at].astype(F32) * pull
        ).astype(BF16)
        return 0

    lax.fori_loop(0, tiles, last, 0, unroll=per)
    store("gtok")
    bends_here()
    total = bends_ref[0]
    for k in range(1, ctx):
        total = total + bends_ref[k]
    ref["bend_out"][...] = total * factor
    tap_all_here()
    sum_all_here()
    link.settle()
    for copy in stores:
        copy.wait()


def finish_kernel(modes, groups, *refs):
    count = len(BIG)
    big, (totals_ref, taps_ref, bend_ref) = refs[:count], refs[count : count + 3]
    outs = refs[count + 3 : 2 * count + 3]
    gain_mr_ref, gain_li_ref, filter_ref, res_ref, rate_ref, *held, flat_ref, come, go = refs[
        2 * count + 3 :
    ]
    arrive = [
        pltpu.make_async_copy(source, hold, come.at[k])
        for k, (source, hold) in enumerate(zip(big, held))
    ]
    leave = [
        pltpu.make_async_copy(hold, target, go.at[k])
        for k, (hold, target) in enumerate(zip(held, outs))
    ]
    for copy in arrive:
        copy.start()
    for before, after in zip(arrive, leave):
        before.wait()
        after.start()
    tiles = gain_mr_ref.shape[0]
    size = modes * tiles
    flat_ref[...] = totals_ref[...].astype(F32)
    for j in range(tiles):
        at = slice(j * LANES, (j + 1) * LANES)
        res_ref[:, at] = flat_ref[pl.ds(j, modes, stride=tiles), :]
        rate_ref[:, at] = flat_ref[pl.ds(size + j, modes, stride=tiles), :]
    filter_ref[...] = taps_ref[...].astype(F32)[:groups]
    gain_mr_ref[...] = bend_ref[:tiles, :]
    gain_li_ref[...] = bend_ref[tiles:, :]
    for copy in leave:
        copy.wait()


def body(
    sizes,
    tokens,
    query_mr,
    key_mr,
    gain_mr,
    filter_mr,
    query_li,
    key_li,
    gain_li,
    log_rates,
    retain,
    residues,
    cotangent,
):
    rows, channels = tokens.shape
    groups, taps = filter_mr.shape
    members = channels // groups
    modes = log_rates.shape[0]
    tiles = channels // LANES
    ctx, tp = sizes["ctx"], sizes["tp"]
    factor = 1.0 / math.sqrt(rows * ctx)
    flat = (modes * tiles, LANES)
    full = (rows, channels)
    sub = min(8, tiles)
    chunks = min(4, tiles)

    given = dict(
        x=tokens, km=key_mr, gm=gain_mr[None, :], cot=cotangent, ql=query_li,
        keep=retain[None, :], lr=log_rates, res=residues, filt=filter_mr, kl=key_li,
        gl=gain_li[None, :], qm=query_mr,
    )
    piece = -(-2 * modes * tiles // (STEP * ctx)) * STEP
    tap_piece = -(-groups // (STEP * ctx)) * STEP
    phases = hops(ctx)
    slots = sum(len(phase) for phase in phases)
    remote = 3 * (tp - 1) + 6 * (ctx - 1) + 2 * chunks + 1 + 2 * slots
    vmem = pltpu.VMEM
    dma = pltpu.SemaphoreType.DMA
    scratch = {name: vmem(given[name].shape, given[name].dtype) for name in INPUTS}
    scratch |= {name: vmem(full, BF16) for name in BIG}
    scratch |= {
        name: vmem(full, BF16)
        for name in ("early", "before", "mix", "prev", "mid", "gconv", "next")
    }
    scratch |= {name: vmem(full, F32) for name in ("conv", "v", "gmid", "gnorm")}
    scratch |= {name: vmem((rows * tiles, LANES), F32) for name in ("g", "u", "y")}
    scratch["adj"] = vmem((rows * (tiles // sub) * modes, sub, LANES), F32)
    scratch |= {
        name: vmem(flat, F32) for name in ("rate", "resid", "pole", "weight", "ahead", "behind")
    }
    for k in range(len(phases)):
        scratch |= {f"lead{k}": vmem(flat, BF16), f"final{k}": vmem(flat, BF16)}
    scratch |= {name: vmem((slots,) + flat, BF16) for name in ("lead_all", "final_all")}
    scratch |= {
        "power": vmem((tp, 8, rows), F32),
        "share": vmem((ctx, 8, rows), F32),
        "sum": vmem((8, rows), F32),
        "sum_before": vmem((8, rows), F32),
        "sums": vmem((tp, 16, rows), F32),
        "inner": vmem((tp, 8, rows), F32),
        "taps": vmem((groups, taps), F32),
        "flip": vmem((groups, taps), F32),
        "fgrad": vmem((groups, taps), F32),
        "bend": vmem((2 * tiles, LANES), F32),
        "bends": vmem((ctx, 2 * tiles, LANES), F32),
        "wsum": vmem(flat, F32),
        "tap_part": vmem((ctx * tap_piece, LANES), BF16),
        "tap_pool": vmem((ctx, tap_piece, LANES), BF16),
        "partf": vmem((ctx * piece, LANES), F32),
        "part": vmem((ctx * piece, LANES), BF16),
        "pool": vmem((ctx, piece, LANES), BF16),
        "send": dma((remote,)),
        "recv": dma((remote,)),
        "load": dma((len(INPUTS),)),
        "store": dma((len(BIG),)),
    }
    names = (
        [name + "_in" for name in INPUTS]
        + [name + "_out" for name in BIG]
        + ["totals_out", "taps_out", "bend_out"]
        + list(scratch)
    )
    anywhere = pl.BlockSpec(memory_space=pl.ANY)
    inside = pl.BlockSpec(memory_space=pltpu.VMEM)
    *big, totals, filters, bend = pl.pallas_call(
        functools.partial(main_kernel, sizes, names, members, factor),
        name="pair",
        out_shape=[jax.ShapeDtypeStruct(full, BF16) for _ in BIG]
        + [
            jax.ShapeDtypeStruct((ctx, piece, LANES), BF16),
            jax.ShapeDtypeStruct((ctx, tap_piece, LANES), BF16),
            jax.ShapeDtypeStruct((2 * tiles, LANES), F32),
        ],
        in_specs=[anywhere] * len(INPUTS),
        out_specs=[anywhere] * len(BIG) + [inside] * 3,
        scratch_shapes=list(scratch.values()),
        compiler_params=pltpu.CompilerParams(
            collective_id=1, has_side_effects=True, vmem_limit_bytes=56 * 2**20
        ),
    )(*[given[name] for name in INPUTS])
    outs = [(full, BF16)] * len(BIG) + [
        ((tiles, LANES), F32), ((tiles, LANES), F32), ((groups, taps), F32),
        ((modes, channels), F32), ((modes, channels), F32),
    ]
    mixed, gtok, gqm, gkm, gql, gkl, ggm, ggl, gfilt, gres, grate = pl.pallas_call(
        functools.partial(finish_kernel, modes, groups),
        name="results",
        out_shape=[jax.ShapeDtypeStruct(s, d) for s, d in outs],
        in_specs=[anywhere] * len(BIG) + [inside] * 3,
        out_specs=[anywhere] * len(BIG) + [inside] * 5,
        scratch_shapes=[vmem(full, BF16)] * len(BIG)
        + [vmem((ctx * piece, LANES), F32), dma((len(BIG),)), dma((len(BIG),))],
    )(
        *big, totals.reshape(ctx * piece, LANES), filters.reshape(ctx * tap_piece, LANES), bend
    )
    return (
        mixed, gtok, gqm, gkm, gql, gkl, ggm.reshape(channels), ggl.reshape(channels),
        gfilt, gres, grate,
    )


def solution(mesh):
    wide, tall, both = P("tp"), P("tp", None), P("ctx", "tp")
    across = P(None, "tp")
    return jax.shard_map(
        functools.partial(body, dict(mesh.shape)),
        mesh=mesh,
        in_specs=(
            both, both, both, wide, tall, both, both, wide, across, P("ctx"), across, both,
        ),
        out_specs=(both,) * 6 + (wide, wide, tall, across, across),
        check_vma=False,
    )
```

```python
import functools
import math

import jax
import jax.numpy as jnp
from jax import lax
from jax.experimental import pallas as pl
from jax.experimental.pallas import tpu as pltpu
from jax.sharding import PartitionSpec as P

EPSILON = 1e-06
LANES = 128
STEP = 16
POOL_LATE = True
MEET_FIRST = True
EARLY = 0
CUT = (2, 1, 1, 0)
F32 = jnp.float32
BF16 = jnp.bfloat16
MESH = pl.DeviceIdType.MESH


class Link:
    def __init__(self, sizes, send, recv):
        self.sizes, self.send, self.recv, self.used = sizes, send, recv, 0
        self.pending = []

    def greet(self, axes):
        barrier = pltpu.get_barrier_semaphore()
        greeted = 0
        for axis in axes:
            me = lax.axis_index(axis)
            for step in range(1, self.sizes[axis]):
                peer = lax.rem(me + step, self.sizes[axis])
                pl.semaphore_signal(barrier, inc=1, device_id={axis: peer}, device_id_type=MESH)
                greeted += 1
        return lambda: pl.semaphore_wait(barrier, greeted)

    def copy(self, source, target, axis, peer):
        slot = self.used
        self.used += 1
        return pltpu.make_async_remote_copy(
            src_ref=source,
            dst_ref=target,
            send_sem=self.send.at[slot],
            recv_sem=self.recv.at[slot],
            device_id={axis: peer},
            device_id_type=MESH,
        )

    def shift(self, source, target, axis, step):
        size = self.sizes[axis]
        me = lax.axis_index(axis)
        copy = self.copy(source, target, axis, lax.rem(me + step + size, size))
        sends = (me + step >= 0) & (me + step < size)
        gets = (me - step >= 0) & (me - step < size)
        pl.when(sends)(copy.start)
        self.pending.append(lambda: pl.when(sends)(copy.wait_send))
        return lambda: pl.when(gets)(copy.wait_recv)

    def gather(self, ref, axis):
        size = self.sizes[axis]
        me = lax.axis_index(axis)
        waits = []
        for step in range(1, size):
            copy = self.copy(ref.at[me], ref.at[me], axis, lax.rem(me + step, size))
            copy.start()
            self.pending.append(copy.wait_send)
            waits.append(copy.wait_recv)
        return lambda: [wait() for wait in waits]

    def scatter(self, source, piece, target, axis):
        size = self.sizes[axis]
        me = lax.axis_index(axis)
        waits = []
        for step in range(1, size):
            peer = lax.rem(me + step, size)
            rows = pl.ds(pl.multiple_of(peer * piece, STEP), piece)
            copy = self.copy(source.at[rows], target.at[me], axis, peer)
            copy.start()
            self.pending.append(copy.wait_send)
            waits.append(copy.wait_recv)
        return lambda: [wait() for wait in waits]

    def settle(self):
        for wait in self.pending:
            wait()


def hops(size):
    phases, cover = [[d for d in (1, 2) if d < size]], 2
    while cover < size:
        phases.append([cover * k for k in (1, 2, 3) if cover * k < size])
        cover *= 4
    return phases


def iota(shape, dim):
    return lax.broadcasted_iota(jnp.int32, shape, dim)


def dot(a, b):
    return jnp.dot(a, b, preferred_element_type=F32)


def column(row):
    return jnp.broadcast_to(row, (LANES, LANES)).T


def row8(partial):
    total = jnp.sum(partial, axis=1, keepdims=True)
    return jnp.broadcast_to(total, partial.shape).T[:8]


def lane_tile(j):
    if isinstance(j, int):
        return pl.ds(j * LANES, LANES)
    return pl.ds(pl.multiple_of(j * LANES, LANES), LANES)


def tree(terms):
    terms = list(terms)
    while len(terms) > 1:
        terms = [functools.reduce(lambda a, c: a + c, terms[k : k + 2]) for k in range(0, len(terms), 2)]
    return terms[0]


def windows(before, here):
    both = jnp.concatenate([before, here], axis=0)
    span = LANES + STEP
    return [both[k * STEP : k * STEP + span] for k in range(LANES // STEP)]


def band(row, back):
    table = pltpu.roll(
        jnp.broadcast_to(row, (STEP, LANES)), 0, 1, stride=1, stride_axis=0
    ).astype(BF16)
    r, c = iota((STEP, LANES), 0), iota((STEP, LANES), 1)
    zero = jnp.zeros_like(table)
    near = c >= r if back else c > r
    first = jnp.where(near, table, zero)
    second = jnp.where(near, zero, table)
    return jnp.concatenate([first, second[:, :STEP]], axis=1)


def filtered(taps, wins, back, owner):
    fold = taps.shape[0]
    left = jnp.concatenate([band(taps[g : g + 1], back) for g in range(fold)], axis=0)
    outs = dot(left, jnp.concatenate(wins, axis=1))
    blocks = []
    for k in range(len(wins)):
        at = slice(k * LANES, (k + 1) * LANES)
        block = outs[:STEP, at]
        for g in range(1, fold):
            block = jnp.where(owner == g, outs[g * STEP : (g + 1) * STEP, at], block)
        blocks.append(block)
    return jnp.concatenate(blocks, axis=0)


def tap_grads(turned, wins, owner, fold):
    count = len(wins)
    zero = jnp.zeros((STEP, LANES), BF16)
    left = jnp.concatenate(
        [
            jnp.concatenate(
                [
                    jnp.where(owner == g, turned[k * STEP : (k + 1) * STEP], zero)
                    for k in range(count)
                ],
                axis=1,
            )
            for g in range(fold)
        ],
        axis=0,
    )
    out = lax.dot_general(
        left, jnp.concatenate(wins, axis=1), (((1,), (1,)), ((), ())), preferred_element_type=F32
    )
    r, c = iota((STEP, LANES), 0), iota((STEP, LANES), 1)
    grads = []
    for g in range(fold):
        pair = out[g * STEP : (g + 1) * STEP]
        rest = jnp.concatenate([pair[:, LANES:], jnp.zeros((STEP, LANES - STEP), F32)], axis=1)
        pair = jnp.where(c > STEP - 1 - r, pair[:, :LANES], rest)
        pair = pltpu.roll(pair, 0, 1, stride=1, stride_axis=0)
        grads.append(jnp.sum(pair, axis=0, keepdims=True))
    return jnp.concatenate(grads, axis=0)


def decay_loss(rate):
    y = 2.0 * rate
    small = 1.0
    for k in range(8, 1, -1):
        small = 1.0 - y / k * small
    return jnp.where(y < 0.25, y * small, 1.0 - jnp.exp(-y))


INPUTS = (
    "lr", "res", "keep", "cot", "ql", "x", "km", "gm", "filt", "qm", "kl", "gl",
)
BIG = ("mixed", "gtok", "gqm", "gkm", "gql", "gkl")


def main_kernel(sizes, names, members, factor, *refs):
    ref = dict(zip(names, refs))
    hbm = {name: ref[name + "_in"] for name in INPUTS}
    ctx, tp = sizes["ctx"], sizes["tp"]
    rows, channels = ref["x"].shape
    modes = ref["lr"].shape[0]
    groups = ref["filt"].shape[0]
    tiles = channels // LANES
    width = channels * tp
    fold = LANES // members
    sub = min(8, tiles)
    bands = tiles // sub
    chunks = min(4, tiles)
    per = tiles // chunks
    span = channels // chunks
    pieces = [slice(c * span, (c + 1) * span) for c in range(chunks)]
    size = modes * tiles
    me_c = lax.axis_index("ctx")
    me_t = lax.axis_index("tp")
    owner = iota((STEP, LANES), 1) // members

    link = Link(sizes, ref["send"], ref["recv"])
    greeted = link.greet(["tp", "ctx"])
    loads = {}
    for k, name in enumerate(INPUTS):
        loads[name] = pltpu.make_async_copy(hbm[name], ref[name], ref["load"].at[k])
        loads[name].start()

    def need(*which):
        for name in which:
            loads[name].wait()

    stores = []

    def store(name):
        k = len(stores)
        copy = pltpu.make_async_copy(ref[name], ref[name + "_out"], ref["store"].at[k])
        copy.start()
        stores.append(copy)

    x_ref, km_ref, gm_ref = ref["x"], ref["km"], ref["gm"]
    early_ref, before_ref = ref["early"], ref["before"]

    need("keep")
    lanes = iota((8, LANES), 1)
    run = jnp.broadcast_to(ref["keep"][...], (8, LANES))
    step = 1
    while step < LANES:
        run = run * jnp.where(lanes >= step, pltpu.roll(run, step, 1), 1.0)
        step *= 2
    share_ref = ref["share"]
    share_ref[me_c] = run
    greeted()
    share_here = link.gather(share_ref, "ctx")
    r_row = run[:1]
    r_col = column(r_row)
    r_end = jnp.broadcast_to(r_row[:, LANES - 1 :], (1, LANES))

    rate_ref, res_ref, pole_ref, weight_ref = ref["rate"], ref["resid"], ref["pole"], ref["weight"]
    need("lr", "res")
    for j in range(tiles):
        at = slice(j * LANES, (j + 1) * LANES)
        rate_ref[pl.ds(j, modes, stride=tiles), :] = jnp.exp(ref["lr"][:, at])
        res_ref[pl.ds(j, modes, stride=tiles), :] = ref["res"][:, at]
    pole_ref[...] = jnp.exp(-rate_ref[...])
    weight_ref[...] = res_ref[...] * jnp.sqrt(decay_loss(rate_ref[...]))

    g_ref, u_ref, y_ref, adj_ref = ref["g"], ref["u"], ref["y"], ref["adj"]
    need("cot", "ql")
    cot_ref, ql_ref = ref["cot"], ref["ql"]
    for j in range(tiles):
        at = slice(j * LANES, (j + 1) * LANES)
        g_ref[pl.ds(j, rows, stride=tiles), :] = (
            cot_ref[:, at].astype(F32) * ql_ref[:, at].astype(F32) * r_col
        )

    def places(b, first, count):
        return [pl.ds((first + n) * tiles + b * sub, sub) for n in range(count)]

    def at_time(t, b):
        return pl.ds(pl.multiple_of(t * tiles + b * sub, sub), sub)

    def sweep(source_ref, reverse, finish):
        for b in range(bands):
            where = places(b, 0, modes)
            pole = [pole_ref[at, :] for at in where]

            def advance(i, states, b=b, pole=pole):
                t = rows - 1 - i if reverse else i
                value = source_ref[at_time(t, b), :]
                return tuple(pole[n] * states[n] + value for n in range(modes))

            states = lax.fori_loop(
                0, rows, advance, tuple(jnp.zeros((sub, LANES), F32) for _ in range(modes)),
                unroll=4,
            )
            for n in range(modes):
                finish(where[n], pole[n], states[n])

    phases = hops(ctx)

    class Carry:
        def __init__(self, sign, send_refs, take_ref, total_ref):
            self.sign, self.send_refs, self.take_ref = sign, send_refs, take_ref
            self.total_ref, self.phase, self.slot = total_ref, 0, 0

        def launch(self):
            self.waits = []
            for distance in phases[self.phase]:
                wait = link.shift(
                    self.send_refs[self.phase], self.take_ref.at[self.slot], "ctx",
                    self.sign * distance,
                )
                self.waits.append((distance, self.slot, wait))
                self.slot += 1

        def share(self, count):
            out = jnp.ones((1, LANES), F32)
            for k in range(1, count + 1):
                who = jnp.clip(me_c - self.sign * k, 0, ctx - 1)
                out = out * jnp.broadcast_to(share_ref[who][:1, LANES - 1 :], (1, LANES))
            return out

        def collect(self):
            total = None if self.phase == 0 else self.total_ref[...]
            for distance, slot, wait in self.waits:
                wait()
                source = me_c - self.sign * distance
                live = (source >= 0) & (source < ctx)
                count = distance - 1 if self.phase == 0 else distance
                part = self.take_ref[slot].astype(F32)
                if count:
                    part = part * (jnp.exp(rate_ref[...] * float(-rows * count)) * self.share(count))
                part = jnp.where(live, part, 0.0)
                total = part if total is None else total + part
            self.total_ref[...] = total
            self.phase += 1
            if self.phase < len(phases):
                self.send_refs[self.phase][...] = total.astype(BF16)
                self.launch()

    lead = [ref[f"lead{k}"] for k in range(len(phases))]
    final = [ref[f"final{k}"] for k in range(len(phases))]

    def leave_lead(at, pole, state):
        lead[0][at, :] = (pole * state).astype(BF16)

    sweep(g_ref, True, leave_lead)
    later = Carry(-1, lead, ref["lead_all"], ref["ahead"])
    later.launch()

    need("x", "km", "gm")
    total = jnp.zeros((rows, LANES), F32)
    halo = []

    def ahead_chunk(c):
        halo.append(
            link.shift(early_ref.at[:, pieces[c]], before_ref.at[:, pieces[c]], "ctx", 1)
        )

    for c in range(chunks):
        def square(j, total):
            at = lane_tile(j)
            x = x_ref[:, at].astype(F32)
            early_ref[:, at] = (km_ref[:, at].astype(F32) * (x * gm_ref[:, at])).astype(BF16)
            return total + x * x

        total = lax.fori_loop(c * per, (c + 1) * per, square, total, unroll=per)
    cut = [chunks * k // 4 for k in CUT]
    for c in range(cut[0]):
        ahead_chunk(c)
    power_ref = ref["power"]
    power_ref[me_t] = row8(total)
    power_here = link.gather(power_ref, "tp")

    need("filt")
    taps = ref["filt"][...]
    k0, k1 = iota((LANES, LANES), 0), iota((LANES, LANES), 1)
    mirror = jnp.where((k0 + k1) % LANES == 0, 1.0, 0.0).astype(BF16)
    ref["taps"][...] = taps.astype(F32)
    ref["flip"][...] = dot(taps, mirror)

    power_here()

    def gathered(of):
        out = of(0)
        for k in range(1, tp):
            out = out + of(k)
        return out

    sum_ref, sum_before_ref = ref["sum"], ref["sum_before"]
    sum_ref[...] = gathered(lambda k: power_ref[k])
    sum_here = link.shift(sum_ref, sum_before_ref, "ctx", 1)
    scale_in = column(lax.rsqrt(sum_ref[:1] / width + EPSILON))
    mix_ref = ref["mix"]

    def mix(j, _):
        at = lane_tile(j)
        normed = x_ref[:, at].astype(F32) * gm_ref[:, at] * scale_in
        mix_ref[:, at] = (km_ref[:, at].astype(F32) * normed).astype(BF16)
        return 0

    lax.fori_loop(0, tiles, mix, 0, unroll=per)

    @pl.when(me_c == 0)
    def _():
        before_ref[...] = jnp.zeros_like(before_ref)
        sum_before_ref[...] = jnp.zeros_like(sum_before_ref)

    sum_here()
    scale_before = column(lax.rsqrt(sum_before_ref[:1] / width + EPSILON))
    need("qm", "kl", "gl")
    qm_ref, kl_ref, gl_ref = ref["qm"], ref["kl"], ref["gl"]
    prev_ref, conv_ref, mid_ref = ref["prev"], ref["conv"], ref["mid"]

    def conv_tile(j, power):
        at = lane_tile(j)
        before = (before_ref[:, at].astype(F32) * scale_before).astype(BF16)
        prev_ref[:, at] = before
        taps = ref["flip"][pl.ds(pl.multiple_of(j * fold, fold), fold), :]
        conv = filtered(taps, windows(before, mix_ref[:, at]), False, owner)
        conv_ref[:, at] = conv
        mid = (x_ref[:, at].astype(F32) + qm_ref[:, at].astype(F32) * conv).astype(BF16)
        mid_ref[:, at] = mid
        mid = mid.astype(F32)
        return power + mid * mid

    def conv_chunk(c, power):
        halo[c]()
        return lax.fori_loop(c * per, (c + 1) * per, conv_tile, power, unroll=per)

    def adjoint():
        ahead_ref = ref["ahead"]
        for b in range(bands):
            where = places(b, 0, modes)
            pole = [pole_ref[at, :] for at in where]
            weight = [weight_ref[at, :] for at in where]

            def keep(t, adj, b=b, weight=weight):
                spot = (t * bands + b) * modes
                for n in range(modes):
                    adj_ref[spot + n] = adj[n]
                y_ref[at_time(t, b), :] = tree(weight[n] * adj[n] for n in range(modes))

            g = g_ref[at_time(rows - 1, b), :]
            start = tuple(ahead_ref[at, :] * r_end + g for at in where)
            keep(rows - 1, start)

            def back(i, adj, b=b, pole=pole, keep=keep):
                t = rows - 2 - i
                g = g_ref[at_time(t, b), :]
                adj = tuple(pole[n] * adj[n] + g for n in range(modes))
                keep(t, adj)
                return adj

            lax.fori_loop(0, rows - 1, back, start, unroll=4)

    inverse = 1.0 / r_col
    v_ref = ref["v"]

    def pulled(c, total):
        for j in range(c * per, (c + 1) * per):
            at = slice(j * LANES, (j + 1) * LANES)
            v = y_ref[pl.ds(j, rows, stride=tiles), :] * inverse
            v_ref[:, at] = v
            here = v * kl_ref[:, at].astype(F32) * gl_ref[:, at] * mid_ref[:, at].astype(F32)
            total = total + here
        return total

    share_here()
    power = jnp.zeros((rows, LANES), F32)
    total = jnp.zeros((rows, LANES), F32)
    later.collect()
    for c in range(cut[0], chunks):
        ahead_chunk(c)
    for c in range(chunks):
        if c == chunks - 1:
            while later.phase < len(phases):
                later.collect()
            adjoint()
            for done in range(c):
                total = pulled(done, total)
        power = conv_chunk(c, power)
    total = pulled(chunks - 1, total)
    sums_ref = ref["sums"]
    sums_ref[me_t] = jnp.concatenate([row8(power), row8(total)], axis=0)
    link.gather(sums_ref, "tp")()
    power = gathered(lambda k: sums_ref[k])
    scale = column(lax.rsqrt(power[:1] / width + EPSILON))
    pull = scale * scale * scale * column(power[8:9]) / width

    gmid_ref, gconv_ref, next_ref = ref["gmid"], ref["gconv"], ref["next"]
    partf_ref = ref["partf"]
    bend_ref = ref["bend"]
    halo = []

    def leave_final(at, pole, state):
        final[0][at, :] = (state * r_end).astype(BF16)

    earlier = Carry(1, final, ref["final_all"], ref["behind"])

    def normed_tile(j):
        at = slice(j * LANES, (j + 1) * LANES)
        normed = mid_ref[:, at].astype(F32) * gl_ref[:, at] * scale
        u_ref[pl.ds(j, rows, stride=tiles), :] = kl_ref[:, at].astype(F32) * normed * inverse
        ref["gkl"][:, at] = (v_ref[:, at] * normed).astype(BF16)

    def behind_chunk(c):
        halo.append(
            link.shift(gconv_ref.at[:, pieces[c]], next_ref.at[:, pieces[c]], "ctx", -1)
        )

    for j in range(tiles):
        if j == cut[1] * per:
            for k in range(tiles):
                normed_tile(k)
            sweep(u_ref, False, leave_final)
            earlier.launch()
        at = slice(j * LANES, (j + 1) * LANES)
        mid = mid_ref[:, at].astype(F32)
        gain = gl_ref[:, at]
        grad = v_ref[:, at] * kl_ref[:, at].astype(F32) * scale
        bend_ref[tiles + j : tiles + j + 1, :] = jnp.sum(grad * mid, axis=0, keepdims=True)
        gmid = cot_ref[:, at].astype(F32) + gain * grad - mid * pull
        gmid_ref[:, at] = gmid
        ref["gqm"][:, at] = (gmid * conv_ref[:, at]).astype(BF16)
        gconv_ref[:, at] = (gmid * qm_ref[:, at].astype(F32)).astype(BF16)
        if j % per == per - 1 and j // per < cut[2]:
            behind_chunk(j // per)
    store("gkl")
    store("gqm")

    half = min(8, modes)
    zero = jnp.zeros((sub, LANES), F32)
    wsum_ref = ref["wsum"]
    def meet_all():
        for b in range(bands):
            def meet(t, sums, b=b):
                u = u_ref[at_time(t, b), :]
                spot = (t * bands + b) * modes
                return tuple(sums[n] + adj_ref[spot + n] * u for n in range(modes))

            sums = lax.fori_loop(0, rows, meet, (zero,) * modes, unroll=4)
            for n, at in enumerate(places(b, 0, modes)):
                wsum_ref[at, :] = sums[n]
    if MEET_FIRST:
        meet_all()
    earlier.collect()
    for c in range(cut[2], chunks):
        behind_chunk(c)
    if not MEET_FIRST:
        meet_all()

    same = (k0 // STEP == k1 // STEP) & (k0 % STEP + k1 % STEP == STEP - 1)
    turn = jnp.where(same, 1.0, 0.0).astype(BF16)
    fgrad_ref = ref["fgrad"]

    def pair_tile(j, _):
        at = lane_tile(j)
        turned = dot(turn, gconv_ref[:, at]).astype(BF16)
        wins = windows(prev_ref[:, at], mix_ref[:, at])
        fgrad_ref[pl.ds(pl.multiple_of(j * fold, fold), fold), :] = tap_grads(
            turned, wins, owner, fold
        )
        return 0

    lax.fori_loop(0, tiles, pair_tile, 0, unroll=per)
    lag = jnp.where((k0 + k1) % LANES == STEP - 1, 1.0, 0.0).astype(BF16)
    tap_part_ref, tap_pool_ref, tap_all_ref = ref["tap_part"], ref["tap_pool"], ref["taps_out"]
    share_rows = tap_pool_ref.shape[1]
    turned_back = dot(fgrad_ref[...].astype(BF16), lag).astype(BF16)
    if groups < ctx * share_rows:
        tap_part_ref[groups:, :] = jnp.zeros((ctx * share_rows - groups, LANES), BF16)
    tap_part_ref[:groups, :] = turned_back
    tap_here = link.scatter(tap_part_ref, share_rows, tap_pool_ref, "ctx")

    @pl.when(me_c == ctx - 1)
    def _():
        next_ref[...] = jnp.zeros_like(next_ref)

    gnorm_ref = ref["gnorm"]
    def back_tile(j, inner):
        at = lane_tile(j)
        taps = ref["taps"][pl.ds(pl.multiple_of(j * fold, fold), fold), :]
        wins = windows(gconv_ref[:, at], next_ref[:, at])
        gmix = filtered(taps, wins, True, owner)
        x = x_ref[:, at].astype(F32)
        gain = gm_ref[:, at]
        ref["gkm"][:, at] = (gmix * (x * gain * scale_in)).astype(BF16)
        gnorm = gmix * km_ref[:, at].astype(F32)
        gnorm_ref[:, at] = gnorm
        drawn = gnorm * x
        bend_ref[pl.ds(j, 1), :] = jnp.sum(drawn * scale_in, axis=0, keepdims=True)
        return inner + drawn * gain

    def back_chunk(c, inner):
        halo[c]()
        return lax.fori_loop(c * per, (c + 1) * per, back_tile, inner, unroll=per)

    def forward():
        behind_ref = ref["behind"]
        for b in range(bands):
            for first in range(0, modes, half):
                where = places(b, first, half)
                pole = [pole_ref[at, :] for at in where]
                weight = [weight_ref[at, :] for at in where]

                def advance(t, carry, b=b, first=first, pole=pole, weight=weight):
                    at = at_time(t, b)
                    u = u_ref[at, :]
                    spot = (t * bands + b) * modes + first
                    states, psum = carry
                    adj = [adj_ref[spot + n] for n in range(half)]
                    psum = tuple(psum[n] + adj[n] * states[n] for n in range(half))
                    states = tuple(pole[n] * states[n] + u for n in range(half))
                    y = tree(weight[n] * states[n] for n in range(half))
                    y_ref[at, :] = y if first == 0 else y_ref[at, :] + y
                    return (states, psum)

                begin = tuple(behind_ref[at, :] for at in where)
                _, psum = lax.fori_loop(0, rows, advance, (begin, (zero,) * half), unroll=4)
                for n in range(half):
                    at = where[n]
                    rate = rate_ref[at, :]
                    resid = res_ref[at, :]
                    spread = jnp.sqrt(decay_loss(rate))
                    slope = rate * resid * jnp.exp(-2.0 * rate) / spread
                    lean = rate * pole[n] * weight[n]
                    wsum = wsum_ref[at, :]
                    partf_ref[at, :] = spread * wsum
                    partf_ref[pl.ds(size + at.start, sub), :] = slope * wsum - lean * psum[n]

    inner = jnp.zeros((rows, LANES), F32)
    early = min(EARLY, chunks - 1)
    for c in range(early):
        inner = back_chunk(c, inner)
    while earlier.phase < len(phases):
        earlier.collect()
    forward()

    part_ref, pool_ref, sum_all_ref = ref["part"], ref["pool"], ref["totals_out"]
    piece = pool_ref.shape[1]
    used = 2 * size
    if used < ctx * piece:
        partf_ref[used:, :] = jnp.zeros((ctx * piece - used, LANES), F32)
    part_ref[...] = partf_ref[...].astype(BF16)
    if cut[3] == 0:
        pool_here = link.scatter(part_ref, piece, pool_ref, "ctx")

    def summed(part_ref, pool_ref, all_ref):
        count = pool_ref.shape[1]
        total = part_ref[pl.ds(pl.multiple_of(me_c * count, STEP), count), :].astype(F32)
        for step in range(1, ctx):
            total = total + pool_ref[lax.rem(me_c + step, ctx)].astype(F32)
        all_ref[me_c] = (total * factor).astype(BF16)
        return link.gather(all_ref, "ctx")

    for c in range(early, chunks):
        inner = back_chunk(c, inner)
        if c + 1 == cut[3]:
            pool_here = link.scatter(part_ref, piece, pool_ref, "ctx")
    inner_ref = ref["inner"]
    inner_ref[me_t] = row8(inner)
    inner_here = link.gather(inner_ref, "tp")
    bends_ref = ref["bends"]
    bends_ref[me_c] = bend_ref[...]
    bends_here = link.gather(bends_ref, "ctx")
    store("gkm")

    tap_here()
    tap_all_here = summed(tap_part_ref, tap_pool_ref, tap_all_ref)
    if not POOL_LATE:
        pool_here()
        sum_all_here = summed(part_ref, pool_ref, sum_all_ref)
    for j in range(tiles):
        at = slice(j * LANES, (j + 1) * LANES)
        conv = y_ref[pl.ds(j, rows, stride=tiles), :] * r_col
        ref["mixed"][:, at] = (
            mid_ref[:, at].astype(F32) + ql_ref[:, at].astype(F32) * conv
        ).astype(BF16)
        ref["gql"][:, at] = (cot_ref[:, at].astype(F32) * conv).astype(BF16)
    store("mixed")
    store("gql")

    if POOL_LATE:
        pool_here()
        sum_all_here = summed(part_ref, pool_ref, sum_all_ref)
    inner_here()
    pull = scale_in * scale_in * scale_in * column(gathered(lambda k: inner_ref[k])[:1]) / width

    def last(j, _):
        at = lane_tile(j)
        ref["gtok"][:, at] = (
            gmid_ref[:, at]
            + gm_ref[:, at] * scale_in * gnorm_ref[:, at]
            - x_ref[:, at].astype(F32) * pull
        ).astype(BF16)
        return 0

    lax.fori_loop(0, tiles, last, 0, unroll=per)
    store("gtok")
    bends_here()
    total = bends_ref[0]
    for k in range(1, ctx):
        total = total + bends_ref[k]
    ref["bend_out"][...] = total * factor
    tap_all_here()
    sum_all_here()
    link.settle()
    for copy in stores:
        copy.wait()


def finish_kernel(modes, groups, *refs):
    count = len(BIG)
    given, outs = refs[: count + 3], refs[count + 3 : 2 * count + 8]
    held, made, (flat_ref, come, go) = (
        refs[2 * count + 8 : 3 * count + 11],
        refs[3 * count + 11 : 3 * count + 16],
        refs[3 * count + 16 :],
    )
    arrive = [
        pltpu.make_async_copy(source, hold, come.at[k])
        for k, (source, hold) in enumerate(zip(given, held))
    ]
    leave = [
        pltpu.make_async_copy(hold, target, go.at[k])
        for k, (hold, target) in enumerate(zip(held[:count] + made, outs))
    ]
    for copy in arrive[count:] + arrive[:count]:
        copy.start()
    totals_ref, taps_ref, bend_ref = held[count:]
    gain_mr_ref, gain_li_ref, filter_ref, res_ref, rate_ref = made
    for copy in arrive[count:]:
        copy.wait()
    tiles = gain_mr_ref.shape[0]
    size = modes * tiles
    flat_ref[...] = totals_ref[...].astype(F32)
    for j in range(tiles):
        at = slice(j * LANES, (j + 1) * LANES)
        res_ref[:, at] = flat_ref[pl.ds(j, modes, stride=tiles), :]
        rate_ref[:, at] = flat_ref[pl.ds(size + j, modes, stride=tiles), :]
    filter_ref[...] = taps_ref[...].astype(F32)[:groups]
    gain_mr_ref[...] = bend_ref[:tiles, :]
    gain_li_ref[...] = bend_ref[tiles:, :]
    for before, after in zip(arrive[:count], leave[:count]):
        before.wait()
        after.start()
    for copy in leave[count:]:
        copy.start()
    for copy in leave:
        copy.wait()


def body(
    sizes,
    tokens,
    query_mr,
    key_mr,
    gain_mr,
    filter_mr,
    query_li,
    key_li,
    gain_li,
    log_rates,
    retain,
    residues,
    cotangent,
):
    rows, channels = tokens.shape
    groups, taps = filter_mr.shape
    members = channels // groups
    modes = log_rates.shape[0]
    tiles = channels // LANES
    ctx, tp = sizes["ctx"], sizes["tp"]
    factor = 1.0 / math.sqrt(rows * ctx)
    flat = (modes * tiles, LANES)
    full = (rows, channels)
    sub = min(8, tiles)
    chunks = min(4, tiles)

    given = dict(
        x=tokens, km=key_mr, gm=gain_mr[None, :], cot=cotangent, ql=query_li,
        keep=retain[None, :], lr=log_rates, res=residues, filt=filter_mr, kl=key_li,
        gl=gain_li[None, :], qm=query_mr,
    )
    piece = -(-2 * modes * tiles // (STEP * ctx)) * STEP
    tap_piece = -(-groups // (STEP * ctx)) * STEP
    phases = hops(ctx)
    slots = sum(len(phase) for phase in phases)
    remote = 3 * (tp - 1) + 6 * (ctx - 1) + 2 * chunks + 1 + 2 * slots
    vmem = pltpu.VMEM
    dma = pltpu.SemaphoreType.DMA
    scratch = {name: vmem(given[name].shape, given[name].dtype) for name in INPUTS}
    scratch |= {name: vmem(full, BF16) for name in BIG}
    scratch |= {
        name: vmem(full, BF16)
        for name in ("early", "before", "mix", "prev", "mid", "gconv", "next")
    }
    scratch |= {name: vmem(full, F32) for name in ("conv", "v", "gmid", "gnorm")}
    scratch |= {name: vmem((rows * tiles, LANES), F32) for name in ("g", "u", "y")}
    scratch["adj"] = vmem((rows * (tiles // sub) * modes, sub, LANES), F32)
    scratch |= {
        name: vmem(flat, F32) for name in ("rate", "resid", "pole", "weight", "ahead", "behind")
    }
    for k in range(len(phases)):
        scratch |= {f"lead{k}": vmem(flat, BF16), f"final{k}": vmem(flat, BF16)}
    scratch |= {name: vmem((slots,) + flat, BF16) for name in ("lead_all", "final_all")}
    scratch |= {
        "power": vmem((tp, 8, rows), F32),
        "share": vmem((ctx, 8, rows), F32),
        "sum": vmem((8, rows), F32),
        "sum_before": vmem((8, rows), F32),
        "sums": vmem((tp, 16, rows), F32),
        "inner": vmem((tp, 8, rows), F32),
        "taps": vmem((groups, taps), F32),
        "flip": vmem((groups, taps), F32),
        "fgrad": vmem((groups, taps), F32),
        "bend": vmem((2 * tiles, LANES), F32),
        "bends": vmem((ctx, 2 * tiles, LANES), F32),
        "wsum": vmem(flat, F32),
        "tap_part": vmem((ctx * tap_piece, LANES), BF16),
        "tap_pool": vmem((ctx, tap_piece, LANES), BF16),
        "partf": vmem((ctx * piece, LANES), F32),
        "part": vmem((ctx * piece, LANES), BF16),
        "pool": vmem((ctx, piece, LANES), BF16),
        "send": dma((remote,)),
        "recv": dma((remote,)),
        "load": dma((len(INPUTS),)),
        "store": dma((len(BIG),)),
    }
    names = (
        [name + "_in" for name in INPUTS]
        + [name + "_out" for name in BIG]
        + ["totals_out", "taps_out", "bend_out"]
        + list(scratch)
    )
    anywhere = pl.BlockSpec(memory_space=pl.ANY)
    inside = pl.BlockSpec(memory_space=pltpu.VMEM)
    *big, totals, filters, bend = pl.pallas_call(
        functools.partial(main_kernel, sizes, names, members, factor),
        name="pair",
        out_shape=[jax.ShapeDtypeStruct(full, BF16) for _ in BIG]
        + [
            jax.ShapeDtypeStruct((ctx, piece, LANES), BF16),
            jax.ShapeDtypeStruct((ctx, tap_piece, LANES), BF16),
            jax.ShapeDtypeStruct((2 * tiles, LANES), F32),
        ],
        in_specs=[anywhere] * len(INPUTS),
        out_specs=[anywhere] * len(BIG) + [inside] * 3,
        scratch_shapes=list(scratch.values()),
        compiler_params=pltpu.CompilerParams(
            collective_id=1, has_side_effects=True, vmem_limit_bytes=56 * 2**20
        ),
    )(*[given[name] for name in INPUTS])
    outs = [(full, BF16)] * len(BIG) + [
        ((tiles, LANES), F32), ((tiles, LANES), F32), ((groups, taps), F32),
        ((modes, channels), F32), ((modes, channels), F32),
    ]
    mixed, gtok, gqm, gkm, gql, gkl, ggm, ggl, gfilt, gres, grate = pl.pallas_call(
        functools.partial(finish_kernel, modes, groups),
        name="results",
        out_shape=[jax.ShapeDtypeStruct(s, d) for s, d in outs],
        in_specs=[anywhere] * (len(BIG) + 3),
        out_specs=[anywhere] * len(outs),
        scratch_shapes=[vmem(full, BF16)] * len(BIG)
        + [
            vmem((ctx * piece, LANES), BF16),
            vmem((ctx * tap_piece, LANES), BF16),
            vmem((2 * tiles, LANES), F32),
        ]
        + [vmem(s, d) for s, d in outs[len(BIG) :]]
        + [vmem((ctx * piece, LANES), F32), dma((len(BIG) + 3,)), dma((len(outs),))],
    )(
        *big, totals.reshape(ctx * piece, LANES), filters.reshape(ctx * tap_piece, LANES), bend
    )
    return (
        mixed, gtok, gqm, gkm, gql, gkl, ggm.reshape(channels), ggl.reshape(channels),
        gfilt, gres, grate,
    )


def solution(mesh):
    wide, tall, both = P("tp"), P("tp", None), P("ctx", "tp")
    across = P(None, "tp")
    return jax.shard_map(
        functools.partial(body, dict(mesh.shape)),
        mesh=mesh,
        in_specs=(
            both, both, both, wide, tall, both, both, wide, across, P("ctx"), across, both,
        ),
        out_specs=(both,) * 6 + (wide, wide, tall, across, across),
        check_vma=False,
    )
```

```python
import functools
import math

import jax
import jax.numpy as jnp
from jax import lax
from jax.experimental import pallas as pl
from jax.experimental.pallas import tpu as pltpu
from jax.sharding import PartitionSpec as P

EPSILON = 1e-06
LANES = 128
STEP = 16
POOL_LATE = True
MEET_FIRST = True
EARLY = 0
CUT = (2, 1, 1, 0)
F32 = jnp.float32
BF16 = jnp.bfloat16
MESH = pl.DeviceIdType.MESH


class Link:
    def __init__(self, sizes, send, recv):
        self.sizes, self.send, self.recv, self.used = sizes, send, recv, 0
        self.pending = []

    def greet(self, axes):
        barrier = pltpu.get_barrier_semaphore()
        greeted = 0
        for axis in axes:
            me = lax.axis_index(axis)
            for step in range(1, self.sizes[axis]):
                peer = lax.rem(me + step, self.sizes[axis])
                pl.semaphore_signal(barrier, inc=1, device_id={axis: peer}, device_id_type=MESH)
                greeted += 1
        return lambda: pl.semaphore_wait(barrier, greeted)

    def copy(self, source, target, axis, peer):
        slot = self.used
        self.used += 1
        return pltpu.make_async_remote_copy(
            src_ref=source,
            dst_ref=target,
            send_sem=self.send.at[slot],
            recv_sem=self.recv.at[slot],
            device_id={axis: peer},
            device_id_type=MESH,
        )

    def shift(self, source, target, axis, step):
        size = self.sizes[axis]
        me = lax.axis_index(axis)
        copy = self.copy(source, target, axis, lax.rem(me + step + size, size))
        sends = (me + step >= 0) & (me + step < size)
        gets = (me - step >= 0) & (me - step < size)
        pl.when(sends)(copy.start)
        self.pending.append(lambda: pl.when(sends)(copy.wait_send))
        return lambda: pl.when(gets)(copy.wait_recv)

    def gather(self, ref, axis):
        size = self.sizes[axis]
        me = lax.axis_index(axis)
        waits = []
        for step in range(1, size):
            copy = self.copy(ref.at[me], ref.at[me], axis, lax.rem(me + step, size))
            copy.start()
            self.pending.append(copy.wait_send)
            waits.append(copy.wait_recv)
        return lambda: [wait() for wait in waits]

    def scatter(self, source, piece, target, axis):
        size = self.sizes[axis]
        me = lax.axis_index(axis)
        waits = []
        for step in range(1, size):
            peer = lax.rem(me + step, size)
            rows = pl.ds(pl.multiple_of(peer * piece, STEP), piece)
            copy = self.copy(source.at[rows], target.at[me], axis, peer)
            copy.start()
            self.pending.append(copy.wait_send)
            waits.append(copy.wait_recv)
        return lambda: [wait() for wait in waits]

    def settle(self):
        for wait in self.pending:
            wait()


def hops(size):
    phases, cover = [[d for d in (1, 2) if d < size]], 2
    while cover < size:
        phases.append([cover * k for k in (1, 2, 3) if cover * k < size])
        cover *= 4
    return phases


def iota(shape, dim):
    return lax.broadcasted_iota(jnp.int32, shape, dim)


def dot(a, b):
    return jnp.dot(a, b, preferred_element_type=F32)


def column(row):
    return jnp.broadcast_to(row, (LANES, LANES)).T


def row8(partial):
    total = jnp.sum(partial, axis=1, keepdims=True)
    return jnp.broadcast_to(total, partial.shape).T[:8]


def lane_tile(j):
    if isinstance(j, int):
        return pl.ds(j * LANES, LANES)
    return pl.ds(pl.multiple_of(j * LANES, LANES), LANES)


def tree(terms):
    terms = list(terms)
    while len(terms) > 1:
        terms = [functools.reduce(lambda a, c: a + c, terms[k : k + 2]) for k in range(0, len(terms), 2)]
    return terms[0]


def windows(before, here):
    both = jnp.concatenate([before, here], axis=0)
    span = LANES + STEP
    return [both[k * STEP : k * STEP + span] for k in range(LANES // STEP)]


def band(row, back):
    table = pltpu.roll(
        jnp.broadcast_to(row, (STEP, LANES)), 0, 1, stride=1, stride_axis=0
    ).astype(BF16)
    r, c = iota((STEP, LANES), 0), iota((STEP, LANES), 1)
    zero = jnp.zeros_like(table)
    near = c >= r if back else c > r
    first = jnp.where(near, table, zero)
    second = jnp.where(near, zero, table)
    return jnp.concatenate([first, second[:, :STEP]], axis=1)


def filtered(taps, wins, back, owner):
    fold = taps.shape[0]
    left = jnp.concatenate([band(taps[g : g + 1], back) for g in range(fold)], axis=0)
    outs = dot(left, jnp.concatenate(wins, axis=1))
    blocks = []
    for k in range(len(wins)):
        at = slice(k * LANES, (k + 1) * LANES)
        block = outs[:STEP, at]
        for g in range(1, fold):
            block = jnp.where(owner == g, outs[g * STEP : (g + 1) * STEP, at], block)
        blocks.append(block)
    return jnp.concatenate(blocks, axis=0)


def tap_grads(turned, wins, owner, fold):
    count = len(wins)
    zero = jnp.zeros((STEP, LANES), BF16)
    left = jnp.concatenate(
        [
            jnp.concatenate(
                [
                    jnp.where(owner == g, turned[k * STEP : (k + 1) * STEP], zero)
                    for k in range(count)
                ],
                axis=1,
            )
            for g in range(fold)
        ],
        axis=0,
    )
    out = lax.dot_general(
        left, jnp.concatenate(wins, axis=1), (((1,), (1,)), ((), ())), preferred_element_type=F32
    )
    r, c = iota((STEP, LANES), 0), iota((STEP, LANES), 1)
    grads = []
    for g in range(fold):
        pair = out[g * STEP : (g + 1) * STEP]
        rest = jnp.concatenate([pair[:, LANES:], jnp.zeros((STEP, LANES - STEP), F32)], axis=1)
        pair = jnp.where(c > STEP - 1 - r, pair[:, :LANES], rest)
        pair = pltpu.roll(pair, 0, 1, stride=1, stride_axis=0)
        grads.append(jnp.sum(pair, axis=0, keepdims=True))
    return jnp.concatenate(grads, axis=0)


def decay_loss(rate):
    y = 2.0 * rate
    small = 1.0
    for k in range(8, 1, -1):
        small = 1.0 - y / k * small
    return jnp.where(y < 0.25, y * small, 1.0 - jnp.exp(-y))


INPUTS = (
    "lr", "res", "keep", "cot", "ql", "x", "km", "gm", "filt", "qm", "kl", "gl",
)
BIG = ("mixed", "gtok", "gqm", "gkm", "gql", "gkl")


def main_kernel(sizes, names, members, factor, *refs):
    ref = dict(zip(names, refs))
    hbm = {name: ref[name + "_in"] for name in INPUTS}
    ctx, tp = sizes["ctx"], sizes["tp"]
    rows, channels = ref["x"].shape
    modes = ref["lr"].shape[0]
    groups = ref["filt"].shape[0]
    tiles = channels // LANES
    width = channels * tp
    fold = LANES // members
    sub = min(8, tiles)
    bands = tiles // sub
    chunks = min(4, tiles)
    per = tiles // chunks
    span = channels // chunks
    pieces = [slice(c * span, (c + 1) * span) for c in range(chunks)]
    size = modes * tiles
    me_c = lax.axis_index("ctx")
    me_t = lax.axis_index("tp")
    owner = iota((STEP, LANES), 1) // members

    link = Link(sizes, ref["send"], ref["recv"])
    greeted = link.greet(["tp", "ctx"])
    loads = {}
    for k, name in enumerate(INPUTS):
        loads[name] = pltpu.make_async_copy(hbm[name], ref[name], ref["load"].at[k])
        loads[name].start()

    def need(*which):
        for name in which:
            loads[name].wait()

    stores = []

    def store(name):
        k = len(stores)
        copy = pltpu.make_async_copy(ref[name], ref[name + "_out"], ref["store"].at[k])
        copy.start()
        stores.append(copy)

    x_ref, km_ref, gm_ref = ref["x"], ref["km"], ref["gm"]
    early_ref, before_ref = ref["early"], ref["before"]

    need("keep")
    lanes = iota((8, LANES), 1)
    run = jnp.broadcast_to(ref["keep"][...], (8, LANES))
    step = 1
    while step < LANES:
        run = run * jnp.where(lanes >= step, pltpu.roll(run, step, 1), 1.0)
        step *= 2
    share_ref = ref["share"]
    share_ref[me_c] = run
    greeted()
    share_here = link.gather(share_ref, "ctx")
    r_row = run[:1]
    r_col = column(r_row)
    r_end = jnp.broadcast_to(r_row[:, LANES - 1 :], (1, LANES))

    rate_ref, res_ref, pole_ref, weight_ref = ref["rate"], ref["resid"], ref["pole"], ref["weight"]
    need("lr", "res")
    for j in range(tiles):
        at = slice(j * LANES, (j + 1) * LANES)
        rate_ref[pl.ds(j, modes, stride=tiles), :] = jnp.exp(ref["lr"][:, at])
        res_ref[pl.ds(j, modes, stride=tiles), :] = ref["res"][:, at]
    pole_ref[...] = jnp.exp(-rate_ref[...])
    weight_ref[...] = res_ref[...] * jnp.sqrt(decay_loss(rate_ref[...]))

    g_ref, u_ref, y_ref, adj_ref = ref["g"], ref["u"], ref["y"], ref["adj"]
    need("cot", "ql")
    cot_ref, ql_ref = ref["cot"], ref["ql"]
    for j in range(tiles):
        at = slice(j * LANES, (j + 1) * LANES)
        g_ref[pl.ds(j, rows, stride=tiles), :] = (
            cot_ref[:, at].astype(F32) * ql_ref[:, at].astype(F32) * r_col
        )

    def places(b, first, count):
        return [pl.ds((first + n) * tiles + b * sub, sub) for n in range(count)]

    def at_time(t, b):
        return pl.ds(pl.multiple_of(t * tiles + b * sub, sub), sub)

    def sweep(source_ref, reverse, finish):
        for b in range(bands):
            where = places(b, 0, modes)
            pole = [pole_ref[at, :] for at in where]

            def advance(i, states, b=b, pole=pole):
                t = rows - 1 - i if reverse else i
                value = source_ref[at_time(t, b), :]
                return tuple(pole[n] * states[n] + value for n in range(modes))

            states = lax.fori_loop(
                0, rows, advance, tuple(jnp.zeros((sub, LANES), F32) for _ in range(modes)),
                unroll=4,
            )
            for n in range(modes):
                finish(where[n], pole[n], states[n])

    phases = hops(ctx)

    class Carry:
        def __init__(self, sign, send_refs, take_ref, total_ref):
            self.sign, self.send_refs, self.take_ref = sign, send_refs, take_ref
            self.total_ref, self.phase, self.slot = total_ref, 0, 0

        def launch(self):
            self.waits = []
            for distance in phases[self.phase]:
                wait = link.shift(
                    self.send_refs[self.phase], self.take_ref.at[self.slot], "ctx",
                    self.sign * distance,
                )
                self.waits.append((distance, self.slot, wait))
                self.slot += 1

        def share(self, count):
            out = jnp.ones((1, LANES), F32)
            for k in range(1, count + 1):
                who = jnp.clip(me_c - self.sign * k, 0, ctx - 1)
                out = out * jnp.broadcast_to(share_ref[who][:1, LANES - 1 :], (1, LANES))
            return out

        def collect(self):
            total = None if self.phase == 0 else self.total_ref[...]
            for distance, slot, wait in self.waits:
                wait()
                source = me_c - self.sign * distance
                live = (source >= 0) & (source < ctx)
                count = distance - 1 if self.phase == 0 else distance
                part = self.take_ref[slot].astype(F32)
                if count:
                    part = part * (jnp.exp(rate_ref[...] * float(-rows * count)) * self.share(count))
                part = jnp.where(live, part, 0.0)
                total = part if total is None else total + part
            self.total_ref[...] = total
            self.phase += 1
            if self.phase < len(phases):
                self.send_refs[self.phase][...] = total.astype(BF16)
                self.launch()

    lead = [ref[f"lead{k}"] for k in range(len(phases))]
    final = [ref[f"final{k}"] for k in range(len(phases))]

    def leave_lead(at, pole, state):
        lead[0][at, :] = (pole * state).astype(BF16)

    sweep(g_ref, True, leave_lead)
    later = Carry(-1, lead, ref["lead_all"], ref["ahead"])
    later.launch()

    need("x", "km", "gm")
    total = jnp.zeros((rows, LANES), F32)
    halo = []

    def ahead_chunk(c):
        halo.append(
            link.shift(early_ref.at[:, pieces[c]], before_ref.at[:, pieces[c]], "ctx", 1)
        )

    for c in range(chunks):
        def square(j, total):
            at = lane_tile(j)
            x = x_ref[:, at].astype(F32)
            early_ref[:, at] = (km_ref[:, at].astype(F32) * (x * gm_ref[:, at])).astype(BF16)
            return total + x * x

        total = lax.fori_loop(c * per, (c + 1) * per, square, total, unroll=per)
    cut = [chunks * k // 4 for k in CUT]
    for c in range(cut[0]):
        ahead_chunk(c)
    power_ref = ref["power"]
    power_ref[me_t] = row8(total)
    power_here = link.gather(power_ref, "tp")

    need("filt")
    taps = ref["filt"][...]
    k0, k1 = iota((LANES, LANES), 0), iota((LANES, LANES), 1)
    mirror = jnp.where((k0 + k1) % LANES == 0, 1.0, 0.0).astype(BF16)
    ref["taps"][...] = taps.astype(F32)
    ref["flip"][...] = dot(taps, mirror)

    power_here()

    def gathered(of):
        out = of(0)
        for k in range(1, tp):
            out = out + of(k)
        return out

    sum_ref, sum_before_ref = ref["sum"], ref["sum_before"]
    sum_ref[...] = gathered(lambda k: power_ref[k])
    sum_here = link.shift(sum_ref, sum_before_ref, "ctx", 1)
    scale_in = column(lax.rsqrt(sum_ref[:1] / width + EPSILON))
    mix_ref = ref["mix"]

    def mix(j, _):
        at = lane_tile(j)
        normed = x_ref[:, at].astype(F32) * gm_ref[:, at] * scale_in
        mix_ref[:, at] = (km_ref[:, at].astype(F32) * normed).astype(BF16)
        return 0

    lax.fori_loop(0, tiles, mix, 0, unroll=per)

    @pl.when(me_c == 0)
    def _():
        before_ref[...] = jnp.zeros_like(before_ref)
        sum_before_ref[...] = jnp.zeros_like(sum_before_ref)

    sum_here()
    scale_before = column(lax.rsqrt(sum_before_ref[:1] / width + EPSILON))
    need("qm", "kl", "gl")
    qm_ref, kl_ref, gl_ref = ref["qm"], ref["kl"], ref["gl"]
    prev_ref, conv_ref, mid_ref = ref["prev"], ref["conv"], ref["mid"]

    def conv_tile(j, power):
        at = lane_tile(j)
        before = (before_ref[:, at].astype(F32) * scale_before).astype(BF16)
        prev_ref[:, at] = before
        taps = ref["flip"][pl.ds(pl.multiple_of(j * fold, fold), fold), :]
        conv = filtered(taps, windows(before, mix_ref[:, at]), False, owner)
        conv_ref[:, at] = conv
        mid = (x_ref[:, at].astype(F32) + qm_ref[:, at].astype(F32) * conv).astype(BF16)
        mid_ref[:, at] = mid
        mid = mid.astype(F32)
        return power + mid * mid

    def conv_chunk(c, power):
        halo[c]()
        return lax.fori_loop(c * per, (c + 1) * per, conv_tile, power, unroll=per)

    def adjoint():
        ahead_ref = ref["ahead"]
        for b in range(bands):
            where = places(b, 0, modes)
            pole = [pole_ref[at, :] for at in where]
            weight = [weight_ref[at, :] for at in where]

            def keep(t, adj, b=b, weight=weight):
                spot = (t * bands + b) * modes
                for n in range(modes):
                    adj_ref[spot + n] = adj[n]
                y_ref[at_time(t, b), :] = tree(weight[n] * adj[n] for n in range(modes))

            g = g_ref[at_time(rows - 1, b), :]
            start = tuple(ahead_ref[at, :] * r_end + g for at in where)
            keep(rows - 1, start)

            def back(i, adj, b=b, pole=pole, keep=keep):
                t = rows - 2 - i
                g = g_ref[at_time(t, b), :]
                adj = tuple(pole[n] * adj[n] + g for n in range(modes))
                keep(t, adj)
                return adj

            lax.fori_loop(0, rows - 1, back, start, unroll=4)

    inverse = 1.0 / r_col
    v_ref = ref["v"]

    def pulled(c, total):
        for j in range(c * per, (c + 1) * per):
            at = slice(j * LANES, (j + 1) * LANES)
            v = y_ref[pl.ds(j, rows, stride=tiles), :] * inverse
            v_ref[:, at] = v
            here = v * kl_ref[:, at].astype(F32) * gl_ref[:, at] * mid_ref[:, at].astype(F32)
            total = total + here
        return total

    share_here()
    power = jnp.zeros((rows, LANES), F32)
    total = jnp.zeros((rows, LANES), F32)
    later.collect()
    for c in range(cut[0], chunks):
        ahead_chunk(c)
    for c in range(chunks):
        if c == chunks - 1:
            while later.phase < len(phases):
                later.collect()
            adjoint()
            for done in range(c):
                total = pulled(done, total)
        power = conv_chunk(c, power)
    total = pulled(chunks - 1, total)
    sums_ref = ref["sums"]
    sums_ref[me_t] = jnp.concatenate([row8(power), row8(total)], axis=0)
    link.gather(sums_ref, "tp")()
    power = gathered(lambda k: sums_ref[k])
    scale = column(lax.rsqrt(power[:1] / width + EPSILON))
    pull = scale * scale * scale * column(power[8:9]) / width

    gmid_ref, gconv_ref, next_ref = ref["gmid"], ref["gconv"], ref["next"]
    partf_ref = ref["partf"]
    bend_ref = ref["bend"]
    halo = []

    def leave_final(at, pole, state):
        final[0][at, :] = (state * r_end).astype(BF16)

    earlier = Carry(1, final, ref["final_all"], ref["behind"])

    def normed_tile(j):
        at = slice(j * LANES, (j + 1) * LANES)
        normed = mid_ref[:, at].astype(F32) * gl_ref[:, at] * scale
        u_ref[pl.ds(j, rows, stride=tiles), :] = kl_ref[:, at].astype(F32) * normed * inverse
        ref["gkl"][:, at] = (v_ref[:, at] * normed).astype(BF16)

    def behind_chunk(c):
        halo.append(
            link.shift(gconv_ref.at[:, pieces[c]], next_ref.at[:, pieces[c]], "ctx", -1)
        )

    for j in range(tiles):
        if j == cut[1] * per:
            for k in range(tiles):
                normed_tile(k)
            sweep(u_ref, False, leave_final)
            earlier.launch()
        at = slice(j * LANES, (j + 1) * LANES)
        mid = mid_ref[:, at].astype(F32)
        gain = gl_ref[:, at]
        grad = v_ref[:, at] * kl_ref[:, at].astype(F32) * scale
        bend_ref[tiles + j : tiles + j + 1, :] = jnp.sum(grad * mid, axis=0, keepdims=True)
        gmid = cot_ref[:, at].astype(F32) + gain * grad - mid * pull
        gmid_ref[:, at] = gmid
        ref["gqm"][:, at] = (gmid * conv_ref[:, at]).astype(BF16)
        gconv_ref[:, at] = (gmid * qm_ref[:, at].astype(F32)).astype(BF16)
        if j % per == per - 1 and j // per < cut[2]:
            behind_chunk(j // per)
    store("gkl")
    store("gqm")

    half = min(8, modes)
    zero = jnp.zeros((sub, LANES), F32)
    wsum_ref = ref["wsum"]
    def meet_all():
        for b in range(bands):
            def meet(t, sums, b=b):
                u = u_ref[at_time(t, b), :]
                spot = (t * bands + b) * modes
                return tuple(sums[n] + adj_ref[spot + n] * u for n in range(modes))

            sums = lax.fori_loop(0, rows, meet, (zero,) * modes, unroll=4)
            for n, at in enumerate(places(b, 0, modes)):
                wsum_ref[at, :] = sums[n]
    if MEET_FIRST:
        meet_all()
    earlier.collect()
    for c in range(cut[2], chunks):
        behind_chunk(c)
    if not MEET_FIRST:
        meet_all()

    same = (k0 // STEP == k1 // STEP) & (k0 % STEP + k1 % STEP == STEP - 1)
    turn = jnp.where(same, 1.0, 0.0).astype(BF16)
    fgrad_ref = ref["fgrad"]

    def pair_tile(j, _):
        at = lane_tile(j)
        turned = dot(turn, gconv_ref[:, at]).astype(BF16)
        wins = windows(prev_ref[:, at], mix_ref[:, at])
        fgrad_ref[pl.ds(pl.multiple_of(j * fold, fold), fold), :] = tap_grads(
            turned, wins, owner, fold
        )
        return 0

    lax.fori_loop(0, tiles, pair_tile, 0, unroll=per)
    lag = jnp.where((k0 + k1) % LANES == STEP - 1, 1.0, 0.0).astype(BF16)
    tap_part_ref, tap_pool_ref, tap_all_ref = ref["tap_part"], ref["tap_pool"], ref["taps_out"]
    share_rows = tap_pool_ref.shape[1]
    turned_back = dot(fgrad_ref[...].astype(BF16), lag).astype(BF16)
    if groups < ctx * share_rows:
        tap_part_ref[groups:, :] = jnp.zeros((ctx * share_rows - groups, LANES), BF16)
    tap_part_ref[:groups, :] = turned_back
    tap_here = link.scatter(tap_part_ref, share_rows, tap_pool_ref, "ctx")

    @pl.when(me_c == ctx - 1)
    def _():
        next_ref[...] = jnp.zeros_like(next_ref)

    gnorm_ref = ref["gnorm"]
    def back_tile(j, inner):
        at = lane_tile(j)
        taps = ref["taps"][pl.ds(pl.multiple_of(j * fold, fold), fold), :]
        wins = windows(gconv_ref[:, at], next_ref[:, at])
        gmix = filtered(taps, wins, True, owner)
        x = x_ref[:, at].astype(F32)
        gain = gm_ref[:, at]
        ref["gkm"][:, at] = (gmix * (x * gain * scale_in)).astype(BF16)
        gnorm = gmix * km_ref[:, at].astype(F32)
        gnorm_ref[:, at] = gnorm
        drawn = gnorm * x
        bend_ref[pl.ds(j, 1), :] = jnp.sum(drawn * scale_in, axis=0, keepdims=True)
        return inner + drawn * gain

    def back_chunk(c, inner):
        halo[c]()
        return lax.fori_loop(c * per, (c + 1) * per, back_tile, inner, unroll=per)

    def forward():
        behind_ref = ref["behind"]
        for b in range(bands):
            for first in range(0, modes, half):
                where = places(b, first, half)
                pole = [pole_ref[at, :] for at in where]
                weight = [weight_ref[at, :] for at in where]

                def advance(t, carry, b=b, first=first, pole=pole, weight=weight):
                    at = at_time(t, b)
                    u = u_ref[at, :]
                    spot = (t * bands + b) * modes + first
                    states, psum = carry
                    adj = [adj_ref[spot + n] for n in range(half)]
                    psum = tuple(psum[n] + adj[n] * states[n] for n in range(half))
                    states = tuple(pole[n] * states[n] + u for n in range(half))
                    y = tree(weight[n] * states[n] for n in range(half))
                    y_ref[at, :] = y if first == 0 else y_ref[at, :] + y
                    return (states, psum)

                begin = tuple(behind_ref[at, :] for at in where)
                _, psum = lax.fori_loop(0, rows, advance, (begin, (zero,) * half), unroll=8)
                for n in range(half):
                    at = where[n]
                    rate = rate_ref[at, :]
                    resid = res_ref[at, :]
                    spread = jnp.sqrt(decay_loss(rate))
                    slope = rate * resid * jnp.exp(-2.0 * rate) / spread
                    lean = rate * pole[n] * weight[n]
                    wsum = wsum_ref[at, :]
                    partf_ref[at, :] = spread * wsum
                    partf_ref[pl.ds(size + at.start, sub), :] = slope * wsum - lean * psum[n]

    inner = jnp.zeros((rows, LANES), F32)
    early = min(EARLY, chunks - 1)
    for c in range(early):
        inner = back_chunk(c, inner)
    while earlier.phase < len(phases):
        earlier.collect()
    forward()

    part_ref, pool_ref, sum_all_ref = ref["part"], ref["pool"], ref["totals_out"]
    piece = pool_ref.shape[1]
    used = 2 * size
    if used < ctx * piece:
        partf_ref[used:, :] = jnp.zeros((ctx * piece - used, LANES), F32)
    part_ref[...] = partf_ref[...].astype(BF16)
    if cut[3] == 0:
        pool_here = link.scatter(part_ref, piece, pool_ref, "ctx")

    def summed(part_ref, pool_ref, all_ref):
        count = pool_ref.shape[1]
        total = part_ref[pl.ds(pl.multiple_of(me_c * count, STEP), count), :].astype(F32)
        for step in range(1, ctx):
            total = total + pool_ref[lax.rem(me_c + step, ctx)].astype(F32)
        all_ref[me_c] = (total * factor).astype(BF16)
        return link.gather(all_ref, "ctx")

    for c in range(early, chunks):
        inner = back_chunk(c, inner)
        if c + 1 == cut[3]:
            pool_here = link.scatter(part_ref, piece, pool_ref, "ctx")
    inner_ref = ref["inner"]
    inner_ref[me_t] = row8(inner)
    inner_here = link.gather(inner_ref, "tp")
    bends_ref = ref["bends"]
    bends_ref[me_c] = bend_ref[...]
    bends_here = link.gather(bends_ref, "ctx")
    store("gkm")

    tap_here()
    tap_all_here = summed(tap_part_ref, tap_pool_ref, tap_all_ref)
    if not POOL_LATE:
        pool_here()
        sum_all_here = summed(part_ref, pool_ref, sum_all_ref)
    for j in range(tiles):
        at = slice(j * LANES, (j + 1) * LANES)
        conv = y_ref[pl.ds(j, rows, stride=tiles), :] * r_col
        ref["mixed"][:, at] = (
            mid_ref[:, at].astype(F32) + ql_ref[:, at].astype(F32) * conv
        ).astype(BF16)
        ref["gql"][:, at] = (cot_ref[:, at].astype(F32) * conv).astype(BF16)
    store("mixed")
    store("gql")

    if POOL_LATE:
        pool_here()
        sum_all_here = summed(part_ref, pool_ref, sum_all_ref)
    inner_here()
    pull = scale_in * scale_in * scale_in * column(gathered(lambda k: inner_ref[k])[:1]) / width

    def last(j, _):
        at = lane_tile(j)
        ref["gtok"][:, at] = (
            gmid_ref[:, at]
            + gm_ref[:, at] * scale_in * gnorm_ref[:, at]
            - x_ref[:, at].astype(F32) * pull
        ).astype(BF16)
        return 0

    lax.fori_loop(0, tiles, last, 0, unroll=per)
    store("gtok")
    bends_here()
    total = bends_ref[0]
    for k in range(1, ctx):
        total = total + bends_ref[k]
    ref["bend_out"][...] = total * factor
    tap_all_here()
    sum_all_here()
    link.settle()
    for copy in stores:
        copy.wait()


def finish_kernel(modes, groups, *refs):
    count = len(BIG)
    given, outs = refs[: count + 3], refs[count + 3 : 2 * count + 8]
    held, made, (flat_ref, come, go) = (
        refs[2 * count + 8 : 3 * count + 11],
        refs[3 * count + 11 : 3 * count + 16],
        refs[3 * count + 16 :],
    )
    arrive = [
        pltpu.make_async_copy(source, hold, come.at[k])
        for k, (source, hold) in enumerate(zip(given, held))
    ]
    leave = [
        pltpu.make_async_copy(hold, target, go.at[k])
        for k, (hold, target) in enumerate(zip(held[:count] + made, outs))
    ]
    for copy in arrive[count:] + arrive[:count]:
        copy.start()
    totals_ref, taps_ref, bend_ref = held[count:]
    gain_mr_ref, gain_li_ref, filter_ref, res_ref, rate_ref = made
    for copy in arrive[count:]:
        copy.wait()
    tiles = gain_mr_ref.shape[0]
    size = modes * tiles
    flat_ref[...] = totals_ref[...].astype(F32)
    for j in range(tiles):
        at = slice(j * LANES, (j + 1) * LANES)
        res_ref[:, at] = flat_ref[pl.ds(j, modes, stride=tiles), :]
        rate_ref[:, at] = flat_ref[pl.ds(size + j, modes, stride=tiles), :]
    filter_ref[...] = taps_ref[...].astype(F32)[:groups]
    gain_mr_ref[...] = bend_ref[:tiles, :]
    gain_li_ref[...] = bend_ref[tiles:, :]
    for before, after in zip(arrive[:count], leave[:count]):
        before.wait()
        after.start()
    for copy in leave[count:]:
        copy.start()
    for copy in leave:
        copy.wait()


def body(
    sizes,
    tokens,
    query_mr,
    key_mr,
    gain_mr,
    filter_mr,
    query_li,
    key_li,
    gain_li,
    log_rates,
    retain,
    residues,
    cotangent,
):
    rows, channels = tokens.shape
    groups, taps = filter_mr.shape
    members = channels // groups
    modes = log_rates.shape[0]
    tiles = channels // LANES
    ctx, tp = sizes["ctx"], sizes["tp"]
    factor = 1.0 / math.sqrt(rows * ctx)
    flat = (modes * tiles, LANES)
    full = (rows, channels)
    sub = min(8, tiles)
    chunks = min(4, tiles)

    given = dict(
        x=tokens, km=key_mr, gm=gain_mr[None, :], cot=cotangent, ql=query_li,
        keep=retain[None, :], lr=log_rates, res=residues, filt=filter_mr, kl=key_li,
        gl=gain_li[None, :], qm=query_mr,
    )
    piece = -(-2 * modes * tiles // (STEP * ctx)) * STEP
    tap_piece = -(-groups // (STEP * ctx)) * STEP
    phases = hops(ctx)
    slots = sum(len(phase) for phase in phases)
    remote = 3 * (tp - 1) + 6 * (ctx - 1) + 2 * chunks + 1 + 2 * slots
    vmem = pltpu.VMEM
    dma = pltpu.SemaphoreType.DMA
    scratch = {name: vmem(given[name].shape, given[name].dtype) for name in INPUTS}
    scratch |= {name: vmem(full, BF16) for name in BIG}
    scratch |= {
        name: vmem(full, BF16)
        for name in ("early", "before", "mix", "prev", "mid", "gconv", "next")
    }
    scratch |= {name: vmem(full, F32) for name in ("conv", "v", "gmid", "gnorm")}
    scratch |= {name: vmem((rows * tiles, LANES), F32) for name in ("g", "u", "y")}
    scratch["adj"] = vmem((rows * (tiles // sub) * modes, sub, LANES), F32)
    scratch |= {
        name: vmem(flat, F32) for name in ("rate", "resid", "pole", "weight", "ahead", "behind")
    }
    for k in range(len(phases)):
        scratch |= {f"lead{k}": vmem(flat, BF16), f"final{k}": vmem(flat, BF16)}
    scratch |= {name: vmem((slots,) + flat, BF16) for name in ("lead_all", "final_all")}
    scratch |= {
        "power": vmem((tp, 8, rows), F32),
        "share": vmem((ctx, 8, rows), F32),
        "sum": vmem((8, rows), F32),
        "sum_before": vmem((8, rows), F32),
        "sums": vmem((tp, 16, rows), F32),
        "inner": vmem((tp, 8, rows), F32),
        "taps": vmem((groups, taps), F32),
        "flip": vmem((groups, taps), F32),
        "fgrad": vmem((groups, taps), F32),
        "bend": vmem((2 * tiles, LANES), F32),
        "bends": vmem((ctx, 2 * tiles, LANES), F32),
        "wsum": vmem(flat, F32),
        "tap_part": vmem((ctx * tap_piece, LANES), BF16),
        "tap_pool": vmem((ctx, tap_piece, LANES), BF16),
        "partf": vmem((ctx * piece, LANES), F32),
        "part": vmem((ctx * piece, LANES), BF16),
        "pool": vmem((ctx, piece, LANES), BF16),
        "send": dma((remote,)),
        "recv": dma((remote,)),
        "load": dma((len(INPUTS),)),
        "store": dma((len(BIG),)),
    }
    names = (
        [name + "_in" for name in INPUTS]
        + [name + "_out" for name in BIG]
        + ["totals_out", "taps_out", "bend_out"]
        + list(scratch)
    )
    anywhere = pl.BlockSpec(memory_space=pl.ANY)
    inside = pl.BlockSpec(memory_space=pltpu.VMEM)
    *big, totals, filters, bend = pl.pallas_call(
        functools.partial(main_kernel, sizes, names, members, factor),
        name="pair",
        out_shape=[jax.ShapeDtypeStruct(full, BF16) for _ in BIG]
        + [
            jax.ShapeDtypeStruct((ctx, piece, LANES), BF16),
            jax.ShapeDtypeStruct((ctx, tap_piece, LANES), BF16),
            jax.ShapeDtypeStruct((2 * tiles, LANES), F32),
        ],
        in_specs=[anywhere] * len(INPUTS),
        out_specs=[anywhere] * len(BIG) + [inside] * 3,
        scratch_shapes=list(scratch.values()),
        compiler_params=pltpu.CompilerParams(
            collective_id=1, has_side_effects=True, vmem_limit_bytes=56 * 2**20
        ),
    )(*[given[name] for name in INPUTS])
    outs = [(full, BF16)] * len(BIG) + [
        ((tiles, LANES), F32), ((tiles, LANES), F32), ((groups, taps), F32),
        ((modes, channels), F32), ((modes, channels), F32),
    ]
    mixed, gtok, gqm, gkm, gql, gkl, ggm, ggl, gfilt, gres, grate = pl.pallas_call(
        functools.partial(finish_kernel, modes, groups),
        name="results",
        out_shape=[jax.ShapeDtypeStruct(s, d) for s, d in outs],
        in_specs=[anywhere] * (len(BIG) + 3),
        out_specs=[anywhere] * len(outs),
        scratch_shapes=[vmem(full, BF16)] * len(BIG)
        + [
            vmem((ctx * piece, LANES), BF16),
            vmem((ctx * tap_piece, LANES), BF16),
            vmem((2 * tiles, LANES), F32),
        ]
        + [vmem(s, d) for s, d in outs[len(BIG) :]]
        + [vmem((ctx * piece, LANES), F32), dma((len(BIG) + 3,)), dma((len(outs),))],
    )(
        *big, totals.reshape(ctx * piece, LANES), filters.reshape(ctx * tap_piece, LANES), bend
    )
    return (
        mixed, gtok, gqm, gkm, gql, gkl, ggm.reshape(channels), ggl.reshape(channels),
        gfilt, gres, grate,
    )


def solution(mesh):
    wide, tall, both = P("tp"), P("tp", None), P("ctx", "tp")
    across = P(None, "tp")
    return jax.shard_map(
        functools.partial(body, dict(mesh.shape)),
        mesh=mesh,
        in_specs=(
            both, both, both, wide, tall, both, both, wide, across, P("ctx"), across, both,
        ),
        out_specs=(both,) * 6 + (wide, wide, tall, across, across),
        check_vma=False,
    )
```

```python
import functools
import math

import jax
import jax.numpy as jnp
from jax import lax
from jax.experimental import pallas as pl
from jax.experimental.pallas import tpu as pltpu
from jax.sharding import PartitionSpec as P

EPSILON = 1e-06
LANES = 128
STEP = 16
POOL_LATE = True
MEET_FIRST = True
EARLY = 0
CUT = (2, 1, 1, 0)
F32 = jnp.float32
BF16 = jnp.bfloat16
MESH = pl.DeviceIdType.MESH


class Link:
    def __init__(self, sizes, send, recv):
        self.sizes, self.send, self.recv, self.used = sizes, send, recv, 0
        self.pending = []

    def greet(self, axes):
        barrier = pltpu.get_barrier_semaphore()
        greeted = 0
        for axis in axes:
            me = lax.axis_index(axis)
            for step in range(1, self.sizes[axis]):
                peer = lax.rem(me + step, self.sizes[axis])
                pl.semaphore_signal(barrier, inc=1, device_id={axis: peer}, device_id_type=MESH)
                greeted += 1
        return lambda: pl.semaphore_wait(barrier, greeted)

    def copy(self, source, target, axis, peer):
        slot = self.used
        self.used += 1
        return pltpu.make_async_remote_copy(
            src_ref=source,
            dst_ref=target,
            send_sem=self.send.at[slot],
            recv_sem=self.recv.at[slot],
            device_id={axis: peer},
            device_id_type=MESH,
        )

    def shift(self, source, target, axis, step):
        size = self.sizes[axis]
        me = lax.axis_index(axis)
        copy = self.copy(source, target, axis, lax.rem(me + step + size, size))
        sends = (me + step >= 0) & (me + step < size)
        gets = (me - step >= 0) & (me - step < size)
        pl.when(sends)(copy.start)
        self.pending.append(lambda: pl.when(sends)(copy.wait_send))
        return lambda: pl.when(gets)(copy.wait_recv)

    def gather(self, ref, axis):
        size = self.sizes[axis]
        me = lax.axis_index(axis)
        waits = []
        for step in range(1, size):
            copy = self.copy(ref.at[me], ref.at[me], axis, lax.rem(me + step, size))
            copy.start()
            self.pending.append(copy.wait_send)
            waits.append(copy.wait_recv)
        return lambda: [wait() for wait in waits]

    def scatter(self, source, piece, target, axis):
        size = self.sizes[axis]
        me = lax.axis_index(axis)
        waits = []
        for step in range(1, size):
            peer = lax.rem(me + step, size)
            rows = pl.ds(pl.multiple_of(peer * piece, STEP), piece)
            copy = self.copy(source.at[rows], target.at[me], axis, peer)
            copy.start()
            self.pending.append(copy.wait_send)
            waits.append(copy.wait_recv)
        return lambda: [wait() for wait in waits]

    def settle(self):
        for wait in self.pending:
            wait()


def hops(size):
    phases, cover = [[d for d in (1, 2) if d < size]], 2
    while cover < size:
        phases.append([cover * k for k in (1, 2, 3) if cover * k < size])
        cover *= 4
    return phases


def iota(shape, dim):
    return lax.broadcasted_iota(jnp.int32, shape, dim)


def dot(a, b):
    return jnp.dot(a, b, preferred_element_type=F32)


def column(row):
    return jnp.broadcast_to(row, (LANES, LANES)).T


def row8(partial):
    total = jnp.sum(partial, axis=1, keepdims=True)
    return jnp.broadcast_to(total, partial.shape).T[:8]


def lane_tile(j):
    if isinstance(j, int):
        return pl.ds(j * LANES, LANES)
    return pl.ds(pl.multiple_of(j * LANES, LANES), LANES)


def tree(terms):
    terms = list(terms)
    while len(terms) > 1:
        terms = [functools.reduce(lambda a, c: a + c, terms[k : k + 2]) for k in range(0, len(terms), 2)]
    return terms[0]


def windows(before, here):
    both = jnp.concatenate([before, here], axis=0)
    span = LANES + STEP
    return [both[k * STEP : k * STEP + span] for k in range(LANES // STEP)]


def band(row, back):
    table = pltpu.roll(
        jnp.broadcast_to(row, (STEP, LANES)), 0, 1, stride=1, stride_axis=0
    ).astype(BF16)
    r, c = iota((STEP, LANES), 0), iota((STEP, LANES), 1)
    zero = jnp.zeros_like(table)
    near = c >= r if back else c > r
    first = jnp.where(near, table, zero)
    second = jnp.where(near, zero, table)
    return jnp.concatenate([first, second[:, :STEP]], axis=1)


def filtered(taps, wins, back, owner):
    fold = taps.shape[0]
    left = jnp.concatenate([band(taps[g : g + 1], back) for g in range(fold)], axis=0)
    outs = dot(left, jnp.concatenate(wins, axis=1))
    blocks = []
    for k in range(len(wins)):
        at = slice(k * LANES, (k + 1) * LANES)
        block = outs[:STEP, at]
        for g in range(1, fold):
            block = jnp.where(owner == g, outs[g * STEP : (g + 1) * STEP, at], block)
        blocks.append(block)
    return jnp.concatenate(blocks, axis=0)


def tap_grads(turned, wins, owner, fold):
    count = len(wins)
    zero = jnp.zeros((STEP, LANES), BF16)
    left = jnp.concatenate(
        [
            jnp.concatenate(
                [
                    jnp.where(owner == g, turned[k * STEP : (k + 1) * STEP], zero)
                    for k in range(count)
                ],
                axis=1,
            )
            for g in range(fold)
        ],
        axis=0,
    )
    out = lax.dot_general(
        left, jnp.concatenate(wins, axis=1), (((1,), (1,)), ((), ())), preferred_element_type=F32
    )
    r, c = iota((STEP, LANES), 0), iota((STEP, LANES), 1)
    grads = []
    for g in range(fold):
        pair = out[g * STEP : (g + 1) * STEP]
        rest = jnp.concatenate([pair[:, LANES:], jnp.zeros((STEP, LANES - STEP), F32)], axis=1)
        pair = jnp.where(c > STEP - 1 - r, pair[:, :LANES], rest)
        pair = pltpu.roll(pair, 0, 1, stride=1, stride_axis=0)
        grads.append(jnp.sum(pair, axis=0, keepdims=True))
    return jnp.concatenate(grads, axis=0)


def decay_loss(rate):
    y = 2.0 * rate
    small = 1.0
    for k in range(8, 1, -1):
        small = 1.0 - y / k * small
    return jnp.where(y < 0.25, y * small, 1.0 - jnp.exp(-y))


INPUTS = (
    "lr", "res", "keep", "cot", "ql", "x", "km", "gm", "filt", "qm", "kl", "gl",
)
BIG = ("mixed", "gtok", "gqm", "gkm", "gql", "gkl")


def main_kernel(sizes, names, members, factor, *refs):
    ref = dict(zip(names, refs))
    hbm = {name: ref[name + "_in"] for name in INPUTS}
    ctx, tp = sizes["ctx"], sizes["tp"]
    rows, channels = ref["x"].shape
    modes = ref["lr"].shape[0]
    groups = ref["filt"].shape[0]
    tiles = channels // LANES
    width = channels * tp
    fold = LANES // members
    sub = min(8, tiles)
    bands = tiles // sub
    chunks = min(4, tiles)
    per = tiles // chunks
    span = channels // chunks
    pieces = [slice(c * span, (c + 1) * span) for c in range(chunks)]
    size = modes * tiles
    me_c = lax.axis_index("ctx")
    me_t = lax.axis_index("tp")
    owner = iota((STEP, LANES), 1) // members

    link = Link(sizes, ref["send"], ref["recv"])
    greeted = link.greet(["tp", "ctx"])
    loads = {}
    for k, name in enumerate(INPUTS):
        loads[name] = pltpu.make_async_copy(hbm[name], ref[name], ref["load"].at[k])
        loads[name].start()

    def need(*which):
        for name in which:
            loads[name].wait()

    stores = []

    def store(name):
        k = len(stores)
        copy = pltpu.make_async_copy(ref[name], ref[name + "_out"], ref["store"].at[k])
        copy.start()
        stores.append(copy)

    x_ref, km_ref, gm_ref = ref["x"], ref["km"], ref["gm"]
    early_ref, before_ref = ref["early"], ref["before"]

    need("keep")
    lanes = iota((8, LANES), 1)
    run = jnp.broadcast_to(ref["keep"][...], (8, LANES))
    step = 1
    while step < LANES:
        run = run * jnp.where(lanes >= step, pltpu.roll(run, step, 1), 1.0)
        step *= 2
    share_ref = ref["share"]
    share_ref[me_c] = run
    greeted()
    share_here = link.gather(share_ref, "ctx")
    r_row = run[:1]
    r_col = column(r_row)
    r_end = jnp.broadcast_to(r_row[:, LANES - 1 :], (1, LANES))

    rate_ref, res_ref, pole_ref, weight_ref = ref["rate"], ref["resid"], ref["pole"], ref["weight"]
    need("lr", "res")
    for j in range(tiles):
        at = slice(j * LANES, (j + 1) * LANES)
        rate_ref[pl.ds(j, modes, stride=tiles), :] = jnp.exp(ref["lr"][:, at])
        res_ref[pl.ds(j, modes, stride=tiles), :] = ref["res"][:, at]
    pole_ref[...] = jnp.exp(-rate_ref[...])
    weight_ref[...] = res_ref[...] * jnp.sqrt(decay_loss(rate_ref[...]))

    g_ref, u_ref, y_ref, adj_ref = ref["g"], ref["u"], ref["y"], ref["adj"]
    need("cot", "ql")
    cot_ref, ql_ref = ref["cot"], ref["ql"]
    for j in range(tiles):
        at = slice(j * LANES, (j + 1) * LANES)
        g_ref[pl.ds(j, rows, stride=tiles), :] = (
            cot_ref[:, at].astype(F32) * ql_ref[:, at].astype(F32) * r_col
        )

    def places(b, first, count):
        return [pl.ds((first + n) * tiles + b * sub, sub) for n in range(count)]

    def at_time(t, b):
        return pl.ds(pl.multiple_of(t * tiles + b * sub, sub), sub)

    def sweep(source_ref, reverse, finish):
        for b in range(bands):
            where = places(b, 0, modes)
            pole = [pole_ref[at, :] for at in where]

            def advance(i, states, b=b, pole=pole):
                t = rows - 1 - i if reverse else i
                value = source_ref[at_time(t, b), :]
                return tuple(pole[n] * states[n] + value for n in range(modes))

            states = lax.fori_loop(
                0, rows, advance, tuple(jnp.zeros((sub, LANES), F32) for _ in range(modes)),
                unroll=4,
            )
            for n in range(modes):
                finish(where[n], pole[n], states[n])

    phases = hops(ctx)

    class Carry:
        def __init__(self, sign, send_refs, take_ref, total_ref):
            self.sign, self.send_refs, self.take_ref = sign, send_refs, take_ref
            self.total_ref, self.phase, self.slot = total_ref, 0, 0

        def launch(self):
            self.waits = []
            for distance in phases[self.phase]:
                wait = link.shift(
                    self.send_refs[self.phase], self.take_ref.at[self.slot], "ctx",
                    self.sign * distance,
                )
                self.waits.append((distance, self.slot, wait))
                self.slot += 1

        def share(self, count):
            out = jnp.ones((1, LANES), F32)
            for k in range(1, count + 1):
                who = jnp.clip(me_c - self.sign * k, 0, ctx - 1)
                out = out * jnp.broadcast_to(share_ref[who][:1, LANES - 1 :], (1, LANES))
            return out

        def collect(self):
            total = None if self.phase == 0 else self.total_ref[...]
            for distance, slot, wait in self.waits:
                wait()
                source = me_c - self.sign * distance
                live = (source >= 0) & (source < ctx)
                count = distance - 1 if self.phase == 0 else distance
                part = self.take_ref[slot].astype(F32)
                if count:
                    part = part * (jnp.exp(rate_ref[...] * float(-rows * count)) * self.share(count))
                part = jnp.where(live, part, 0.0)
                total = part if total is None else total + part
            self.total_ref[...] = total
            self.phase += 1
            if self.phase < len(phases):
                self.send_refs[self.phase][...] = total.astype(BF16)
                self.launch()

    lead = [ref[f"lead{k}"] for k in range(len(phases))]
    final = [ref[f"final{k}"] for k in range(len(phases))]

    def leave_lead(at, pole, state):
        lead[0][at, :] = (pole * state).astype(BF16)

    sweep(g_ref, True, leave_lead)
    later = Carry(-1, lead, ref["lead_all"], ref["ahead"])
    later.launch()

    need("x", "km", "gm")
    total = jnp.zeros((rows, LANES), F32)
    halo = []

    def ahead_chunk(c):
        halo.append(
            link.shift(early_ref.at[:, pieces[c]], before_ref.at[:, pieces[c]], "ctx", 1)
        )

    for c in range(chunks):
        def square(j, total):
            at = lane_tile(j)
            x = x_ref[:, at].astype(F32)
            early_ref[:, at] = (km_ref[:, at].astype(F32) * (x * gm_ref[:, at])).astype(BF16)
            return total + x * x

        total = lax.fori_loop(c * per, (c + 1) * per, square, total, unroll=per)
    cut = [chunks * k // 4 for k in CUT]
    for c in range(cut[0]):
        ahead_chunk(c)
    power_ref = ref["power"]
    power_ref[me_t] = row8(total)
    power_here = link.gather(power_ref, "tp")

    need("filt")
    taps = ref["filt"][...]
    k0, k1 = iota((LANES, LANES), 0), iota((LANES, LANES), 1)
    mirror = jnp.where((k0 + k1) % LANES == 0, 1.0, 0.0).astype(BF16)
    ref["taps"][...] = taps.astype(F32)
    ref["flip"][...] = dot(taps, mirror)

    power_here()

    def gathered(of):
        out = of(0)
        for k in range(1, tp):
            out = out + of(k)
        return out

    sum_ref, sum_before_ref = ref["sum"], ref["sum_before"]
    sum_ref[...] = gathered(lambda k: power_ref[k])
    sum_here = link.shift(sum_ref, sum_before_ref, "ctx", 1)
    scale_in = column(lax.rsqrt(sum_ref[:1] / width + EPSILON))
    mix_ref = ref["mix"]

    def mix(j, _):
        at = lane_tile(j)
        normed = x_ref[:, at].astype(F32) * gm_ref[:, at] * scale_in
        mix_ref[:, at] = (km_ref[:, at].astype(F32) * normed).astype(BF16)
        return 0

    lax.fori_loop(0, tiles, mix, 0, unroll=per)

    @pl.when(me_c == 0)
    def _():
        before_ref[...] = jnp.zeros_like(before_ref)
        sum_before_ref[...] = jnp.zeros_like(sum_before_ref)

    sum_here()
    scale_before = column(lax.rsqrt(sum_before_ref[:1] / width + EPSILON))
    need("qm", "kl", "gl")
    qm_ref, kl_ref, gl_ref = ref["qm"], ref["kl"], ref["gl"]
    prev_ref, conv_ref, mid_ref = ref["prev"], ref["conv"], ref["mid"]

    def conv_tile(j, power):
        at = lane_tile(j)
        before = (before_ref[:, at].astype(F32) * scale_before).astype(BF16)
        prev_ref[:, at] = before
        taps = ref["flip"][pl.ds(pl.multiple_of(j * fold, fold), fold), :]
        conv = filtered(taps, windows(before, mix_ref[:, at]), False, owner)
        conv_ref[:, at] = conv
        mid = (x_ref[:, at].astype(F32) + qm_ref[:, at].astype(F32) * conv).astype(BF16)
        mid_ref[:, at] = mid
        mid = mid.astype(F32)
        return power + mid * mid

    def conv_chunk(c, power):
        halo[c]()
        return lax.fori_loop(c * per, (c + 1) * per, conv_tile, power, unroll=per)

    def adjoint():
        ahead_ref = ref["ahead"]
        for b in range(bands):
            where = places(b, 0, modes)
            pole = [pole_ref[at, :] for at in where]
            weight = [weight_ref[at, :] for at in where]

            def keep(t, adj, b=b, weight=weight):
                spot = (t * bands + b) * modes
                for n in range(modes):
                    adj_ref[spot + n] = adj[n]
                y_ref[at_time(t, b), :] = tree(weight[n] * adj[n] for n in range(modes))

            g = g_ref[at_time(rows - 1, b), :]
            start = tuple(ahead_ref[at, :] * r_end + g for at in where)
            keep(rows - 1, start)

            def back(i, adj, b=b, pole=pole, keep=keep):
                t = rows - 2 - i
                g = g_ref[at_time(t, b), :]
                adj = tuple(pole[n] * adj[n] + g for n in range(modes))
                keep(t, adj)
                return adj

            lax.fori_loop(0, rows - 1, back, start, unroll=8)

    inverse = 1.0 / r_col
    v_ref = ref["v"]

    def pulled(c, total):
        for j in range(c * per, (c + 1) * per):
            at = slice(j * LANES, (j + 1) * LANES)
            v = y_ref[pl.ds(j, rows, stride=tiles), :] * inverse
            v_ref[:, at] = v
            here = v * kl_ref[:, at].astype(F32) * gl_ref[:, at] * mid_ref[:, at].astype(F32)
            total = total + here
        return total

    share_here()
    power = jnp.zeros((rows, LANES), F32)
    total = jnp.zeros((rows, LANES), F32)
    later.collect()
    for c in range(cut[0], chunks):
        ahead_chunk(c)
    for c in range(chunks):
        if c == chunks - 1:
            while later.phase < len(phases):
                later.collect()
            adjoint()
            for done in range(c):
                total = pulled(done, total)
        power = conv_chunk(c, power)
    total = pulled(chunks - 1, total)
    sums_ref = ref["sums"]
    sums_ref[me_t] = jnp.concatenate([row8(power), row8(total)], axis=0)
    link.gather(sums_ref, "tp")()
    power = gathered(lambda k: sums_ref[k])
    scale = column(lax.rsqrt(power[:1] / width + EPSILON))
    pull = scale * scale * scale * column(power[8:9]) / width

    gmid_ref, gconv_ref, next_ref = ref["gmid"], ref["gconv"], ref["next"]
    partf_ref = ref["partf"]
    bend_ref = ref["bend"]
    halo = []

    def leave_final(at, pole, state):
        final[0][at, :] = (state * r_end).astype(BF16)

    earlier = Carry(1, final, ref["final_all"], ref["behind"])

    def normed_tile(j):
        at = slice(j * LANES, (j + 1) * LANES)
        normed = mid_ref[:, at].astype(F32) * gl_ref[:, at] * scale
        u_ref[pl.ds(j, rows, stride=tiles), :] = kl_ref[:, at].astype(F32) * normed * inverse
        ref["gkl"][:, at] = (v_ref[:, at] * normed).astype(BF16)

    def behind_chunk(c):
        halo.append(
            link.shift(gconv_ref.at[:, pieces[c]], next_ref.at[:, pieces[c]], "ctx", -1)
        )

    for j in range(tiles):
        if j == cut[1] * per:
            for k in range(tiles):
                normed_tile(k)
            sweep(u_ref, False, leave_final)
            earlier.launch()
        at = slice(j * LANES, (j + 1) * LANES)
        mid = mid_ref[:, at].astype(F32)
        gain = gl_ref[:, at]
        grad = v_ref[:, at] * kl_ref[:, at].astype(F32) * scale
        bend_ref[tiles + j : tiles + j + 1, :] = jnp.sum(grad * mid, axis=0, keepdims=True)
        gmid = cot_ref[:, at].astype(F32) + gain * grad - mid * pull
        gmid_ref[:, at] = gmid
        ref["gqm"][:, at] = (gmid * conv_ref[:, at]).astype(BF16)
        gconv_ref[:, at] = (gmid * qm_ref[:, at].astype(F32)).astype(BF16)
        if j % per == per - 1 and j // per < cut[2]:
            behind_chunk(j // per)
    store("gkl")
    store("gqm")

    half = min(8, modes)
    zero = jnp.zeros((sub, LANES), F32)
    wsum_ref = ref["wsum"]
    def meet_all():
        for b in range(bands):
            def meet(t, sums, b=b):
                u = u_ref[at_time(t, b), :]
                spot = (t * bands + b) * modes
                return tuple(sums[n] + adj_ref[spot + n] * u for n in range(modes))

            sums = lax.fori_loop(0, rows, meet, (zero,) * modes, unroll=4)
            for n, at in enumerate(places(b, 0, modes)):
                wsum_ref[at, :] = sums[n]
    if MEET_FIRST:
        meet_all()
    earlier.collect()
    for c in range(cut[2], chunks):
        behind_chunk(c)
    if not MEET_FIRST:
        meet_all()

    same = (k0 // STEP == k1 // STEP) & (k0 % STEP + k1 % STEP == STEP - 1)
    turn = jnp.where(same, 1.0, 0.0).astype(BF16)
    fgrad_ref = ref["fgrad"]

    def pair_tile(j, _):
        at = lane_tile(j)
        turned = dot(turn, gconv_ref[:, at]).astype(BF16)
        wins = windows(prev_ref[:, at], mix_ref[:, at])
        fgrad_ref[pl.ds(pl.multiple_of(j * fold, fold), fold), :] = tap_grads(
            turned, wins, owner, fold
        )
        return 0

    lax.fori_loop(0, tiles, pair_tile, 0, unroll=per)
    lag = jnp.where((k0 + k1) % LANES == STEP - 1, 1.0, 0.0).astype(BF16)
    tap_part_ref, tap_pool_ref, tap_all_ref = ref["tap_part"], ref["tap_pool"], ref["taps_out"]
    share_rows = tap_pool_ref.shape[1]
    turned_back = dot(fgrad_ref[...].astype(BF16), lag).astype(BF16)
    if groups < ctx * share_rows:
        tap_part_ref[groups:, :] = jnp.zeros((ctx * share_rows - groups, LANES), BF16)
    tap_part_ref[:groups, :] = turned_back
    tap_here = link.scatter(tap_part_ref, share_rows, tap_pool_ref, "ctx")

    @pl.when(me_c == ctx - 1)
    def _():
        next_ref[...] = jnp.zeros_like(next_ref)

    gnorm_ref = ref["gnorm"]
    def back_tile(j, inner):
        at = lane_tile(j)
        taps = ref["taps"][pl.ds(pl.multiple_of(j * fold, fold), fold), :]
        wins = windows(gconv_ref[:, at], next_ref[:, at])
        gmix = filtered(taps, wins, True, owner)
        x = x_ref[:, at].astype(F32)
        gain = gm_ref[:, at]
        ref["gkm"][:, at] = (gmix * (x * gain * scale_in)).astype(BF16)
        gnorm = gmix * km_ref[:, at].astype(F32)
        gnorm_ref[:, at] = gnorm
        drawn = gnorm * x
        bend_ref[pl.ds(j, 1), :] = jnp.sum(drawn * scale_in, axis=0, keepdims=True)
        return inner + drawn * gain

    def back_chunk(c, inner):
        halo[c]()
        return lax.fori_loop(c * per, (c + 1) * per, back_tile, inner, unroll=per)

    def forward():
        behind_ref = ref["behind"]
        for b in range(bands):
            for first in range(0, modes, half):
                where = places(b, first, half)
                pole = [pole_ref[at, :] for at in where]
                weight = [weight_ref[at, :] for at in where]

                def advance(t, carry, b=b, first=first, pole=pole, weight=weight):
                    at = at_time(t, b)
                    u = u_ref[at, :]
                    spot = (t * bands + b) * modes + first
                    states, psum = carry
                    adj = [adj_ref[spot + n] for n in range(half)]
                    psum = tuple(psum[n] + adj[n] * states[n] for n in range(half))
                    states = tuple(pole[n] * states[n] + u for n in range(half))
                    y = tree(weight[n] * states[n] for n in range(half))
                    y_ref[at, :] = y if first == 0 else y_ref[at, :] + y
                    return (states, psum)

                begin = tuple(behind_ref[at, :] for at in where)
                _, psum = lax.fori_loop(0, rows, advance, (begin, (zero,) * half), unroll=8)
                for n in range(half):
                    at = where[n]
                    rate = rate_ref[at, :]
                    resid = res_ref[at, :]
                    spread = jnp.sqrt(decay_loss(rate))
                    slope = rate * resid * jnp.exp(-2.0 * rate) / spread
                    lean = rate * pole[n] * weight[n]
                    wsum = wsum_ref[at, :]
                    partf_ref[at, :] = spread * wsum
                    partf_ref[pl.ds(size + at.start, sub), :] = slope * wsum - lean * psum[n]

    inner = jnp.zeros((rows, LANES), F32)
    early = min(EARLY, chunks - 1)
    for c in range(early):
        inner = back_chunk(c, inner)
    while earlier.phase < len(phases):
        earlier.collect()
    forward()

    part_ref, pool_ref, sum_all_ref = ref["part"], ref["pool"], ref["totals_out"]
    piece = pool_ref.shape[1]
    used = 2 * size
    if used < ctx * piece:
        partf_ref[used:, :] = jnp.zeros((ctx * piece - used, LANES), F32)
    part_ref[...] = partf_ref[...].astype(BF16)
    if cut[3] == 0:
        pool_here = link.scatter(part_ref, piece, pool_ref, "ctx")

    def summed(part_ref, pool_ref, all_ref):
        count = pool_ref.shape[1]
        total = part_ref[pl.ds(pl.multiple_of(me_c * count, STEP), count), :].astype(F32)
        for step in range(1, ctx):
            total = total + pool_ref[lax.rem(me_c + step, ctx)].astype(F32)
        all_ref[me_c] = (total * factor).astype(BF16)
        return link.gather(all_ref, "ctx")

    for c in range(early, chunks):
        inner = back_chunk(c, inner)
        if c + 1 == cut[3]:
            pool_here = link.scatter(part_ref, piece, pool_ref, "ctx")
    inner_ref = ref["inner"]
    inner_ref[me_t] = row8(inner)
    inner_here = link.gather(inner_ref, "tp")
    bends_ref = ref["bends"]
    bends_ref[me_c] = bend_ref[...]
    bends_here = link.gather(bends_ref, "ctx")
    store("gkm")

    tap_here()
    tap_all_here = summed(tap_part_ref, tap_pool_ref, tap_all_ref)
    if not POOL_LATE:
        pool_here()
        sum_all_here = summed(part_ref, pool_ref, sum_all_ref)
    for j in range(tiles):
        at = slice(j * LANES, (j + 1) * LANES)
        conv = y_ref[pl.ds(j, rows, stride=tiles), :] * r_col
        ref["mixed"][:, at] = (
            mid_ref[:, at].astype(F32) + ql_ref[:, at].astype(F32) * conv
        ).astype(BF16)
        ref["gql"][:, at] = (cot_ref[:, at].astype(F32) * conv).astype(BF16)
    store("mixed")
    store("gql")

    if POOL_LATE:
        pool_here()
        sum_all_here = summed(part_ref, pool_ref, sum_all_ref)
    inner_here()
    pull = scale_in * scale_in * scale_in * column(gathered(lambda k: inner_ref[k])[:1]) / width

    def last(j, _):
        at = lane_tile(j)
        ref["gtok"][:, at] = (
            gmid_ref[:, at]
            + gm_ref[:, at] * scale_in * gnorm_ref[:, at]
            - x_ref[:, at].astype(F32) * pull
        ).astype(BF16)
        return 0

    lax.fori_loop(0, tiles, last, 0, unroll=per)
    store("gtok")
    bends_here()
    total = bends_ref[0]
    for k in range(1, ctx):
        total = total + bends_ref[k]
    ref["bend_out"][...] = total * factor
    tap_all_here()
    sum_all_here()
    link.settle()
    for copy in stores:
        copy.wait()


def finish_kernel(modes, groups, *refs):
    count = len(BIG)
    given, outs = refs[: count + 3], refs[count + 3 : 2 * count + 8]
    held, made, (flat_ref, come, go) = (
        refs[2 * count + 8 : 3 * count + 11],
        refs[3 * count + 11 : 3 * count + 16],
        refs[3 * count + 16 :],
    )
    arrive = [
        pltpu.make_async_copy(source, hold, come.at[k])
        for k, (source, hold) in enumerate(zip(given, held))
    ]
    leave = [
        pltpu.make_async_copy(hold, target, go.at[k])
        for k, (hold, target) in enumerate(zip(held[:count] + made, outs))
    ]
    for copy in arrive[count:] + arrive[:count]:
        copy.start()
    totals_ref, taps_ref, bend_ref = held[count:]
    gain_mr_ref, gain_li_ref, filter_ref, res_ref, rate_ref = made
    for copy in arrive[count:]:
        copy.wait()
    tiles = gain_mr_ref.shape[0]
    size = modes * tiles
    flat_ref[...] = totals_ref[...].astype(F32)
    for j in range(tiles):
        at = slice(j * LANES, (j + 1) * LANES)
        res_ref[:, at] = flat_ref[pl.ds(j, modes, stride=tiles), :]
        rate_ref[:, at] = flat_ref[pl.ds(size + j, modes, stride=tiles), :]
    filter_ref[...] = taps_ref[...].astype(F32)[:groups]
    gain_mr_ref[...] = bend_ref[:tiles, :]
    gain_li_ref[...] = bend_ref[tiles:, :]
    for before, after in zip(arrive[:count], leave[:count]):
        before.wait()
        after.start()
    for copy in leave[count:]:
        copy.start()
    for copy in leave:
        copy.wait()


def body(
    sizes,
    tokens,
    query_mr,
    key_mr,
    gain_mr,
    filter_mr,
    query_li,
    key_li,
    gain_li,
    log_rates,
    retain,
    residues,
    cotangent,
):
    rows, channels = tokens.shape
    groups, taps = filter_mr.shape
    members = channels // groups
    modes = log_rates.shape[0]
    tiles = channels // LANES
    ctx, tp = sizes["ctx"], sizes["tp"]
    factor = 1.0 / math.sqrt(rows * ctx)
    flat = (modes * tiles, LANES)
    full = (rows, channels)
    sub = min(8, tiles)
    chunks = min(4, tiles)

    given = dict(
        x=tokens, km=key_mr, gm=gain_mr[None, :], cot=cotangent, ql=query_li,
        keep=retain[None, :], lr=log_rates, res=residues, filt=filter_mr, kl=key_li,
        gl=gain_li[None, :], qm=query_mr,
    )
    piece = -(-2 * modes * tiles // (STEP * ctx)) * STEP
    tap_piece = -(-groups // (STEP * ctx)) * STEP
    phases = hops(ctx)
    slots = sum(len(phase) for phase in phases)
    remote = 3 * (tp - 1) + 6 * (ctx - 1) + 2 * chunks + 1 + 2 * slots
    vmem = pltpu.VMEM
    dma = pltpu.SemaphoreType.DMA
    scratch = {name: vmem(given[name].shape, given[name].dtype) for name in INPUTS}
    scratch |= {name: vmem(full, BF16) for name in BIG}
    scratch |= {
        name: vmem(full, BF16)
        for name in ("early", "before", "mix", "prev", "mid", "gconv", "next")
    }
    scratch |= {name: vmem(full, F32) for name in ("conv", "v", "gmid", "gnorm")}
    scratch |= {name: vmem((rows * tiles, LANES), F32) for name in ("g", "u", "y")}
    scratch["adj"] = vmem((rows * (tiles // sub) * modes, sub, LANES), F32)
    scratch |= {
        name: vmem(flat, F32) for name in ("rate", "resid", "pole", "weight", "ahead", "behind")
    }
    for k in range(len(phases)):
        scratch |= {f"lead{k}": vmem(flat, BF16), f"final{k}": vmem(flat, BF16)}
    scratch |= {name: vmem((slots,) + flat, BF16) for name in ("lead_all", "final_all")}
    scratch |= {
        "power": vmem((tp, 8, rows), F32),
        "share": vmem((ctx, 8, rows), F32),
        "sum": vmem((8, rows), F32),
        "sum_before": vmem((8, rows), F32),
        "sums": vmem((tp, 16, rows), F32),
        "inner": vmem((tp, 8, rows), F32),
        "taps": vmem((groups, taps), F32),
        "flip": vmem((groups, taps), F32),
        "fgrad": vmem((groups, taps), F32),
        "bend": vmem((2 * tiles, LANES), F32),
        "bends": vmem((ctx, 2 * tiles, LANES), F32),
        "wsum": vmem(flat, F32),
        "tap_part": vmem((ctx * tap_piece, LANES), BF16),
        "tap_pool": vmem((ctx, tap_piece, LANES), BF16),
        "partf": vmem((ctx * piece, LANES), F32),
        "part": vmem((ctx * piece, LANES), BF16),
        "pool": vmem((ctx, piece, LANES), BF16),
        "send": dma((remote,)),
        "recv": dma((remote,)),
        "load": dma((len(INPUTS),)),
        "store": dma((len(BIG),)),
    }
    names = (
        [name + "_in" for name in INPUTS]
        + [name + "_out" for name in BIG]
        + ["totals_out", "taps_out", "bend_out"]
        + list(scratch)
    )
    anywhere = pl.BlockSpec(memory_space=pl.ANY)
    inside = pl.BlockSpec(memory_space=pltpu.VMEM)
    *big, totals, filters, bend = pl.pallas_call(
        functools.partial(main_kernel, sizes, names, members, factor),
        name="pair",
        out_shape=[jax.ShapeDtypeStruct(full, BF16) for _ in BIG]
        + [
            jax.ShapeDtypeStruct((ctx, piece, LANES), BF16),
            jax.ShapeDtypeStruct((ctx, tap_piece, LANES), BF16),
            jax.ShapeDtypeStruct((2 * tiles, LANES), F32),
        ],
        in_specs=[anywhere] * len(INPUTS),
        out_specs=[anywhere] * len(BIG) + [inside] * 3,
        scratch_shapes=list(scratch.values()),
        compiler_params=pltpu.CompilerParams(
            collective_id=1, has_side_effects=True, vmem_limit_bytes=56 * 2**20
        ),
    )(*[given[name] for name in INPUTS])
    outs = [(full, BF16)] * len(BIG) + [
        ((tiles, LANES), F32), ((tiles, LANES), F32), ((groups, taps), F32),
        ((modes, channels), F32), ((modes, channels), F32),
    ]
    mixed, gtok, gqm, gkm, gql, gkl, ggm, ggl, gfilt, gres, grate = pl.pallas_call(
        functools.partial(finish_kernel, modes, groups),
        name="results",
        out_shape=[jax.ShapeDtypeStruct(s, d) for s, d in outs],
        in_specs=[anywhere] * (len(BIG) + 3),
        out_specs=[anywhere] * len(outs),
        scratch_shapes=[vmem(full, BF16)] * len(BIG)
        + [
            vmem((ctx * piece, LANES), BF16),
            vmem((ctx * tap_piece, LANES), BF16),
            vmem((2 * tiles, LANES), F32),
        ]
        + [vmem(s, d) for s, d in outs[len(BIG) :]]
        + [vmem((ctx * piece, LANES), F32), dma((len(BIG) + 3,)), dma((len(outs),))],
    )(
        *big, totals.reshape(ctx * piece, LANES), filters.reshape(ctx * tap_piece, LANES), bend
    )
    return (
        mixed, gtok, gqm, gkm, gql, gkl, ggm.reshape(channels), ggl.reshape(channels),
        gfilt, gres, grate,
    )


def solution(mesh):
    wide, tall, both = P("tp"), P("tp", None), P("ctx", "tp")
    across = P(None, "tp")
    return jax.shard_map(
        functools.partial(body, dict(mesh.shape)),
        mesh=mesh,
        in_specs=(
            both, both, both, wide, tall, both, both, wide, across, P("ctx"), across, both,
        ),
        out_specs=(both,) * 6 + (wide, wide, tall, across, across),
        check_vma=False,
    )
```
